768 devices in a mesh: dom: 16 (over y, core), event: 48 (over x, z).
Axes of the slice: x: 4, y: 8, z: 12, core: 2. Of those that a mesh axis runs over, the one named last changes fastest.
Arguments:
- adjoint_state: float32 [48, 9, 64, 12288], P('event', None, None, 'dom'), may hold values from -6 to 6
- forward_velocity: float32 [48, 3, 3, 64, 12288], P('event', None, None, None, 'dom'), may hold values from -6 to 6
- density: float32 [64, 12288], P(None, 'dom'), may hold values from 1 to 3
- lame_lambda: float32 [64, 12288], P(None, 'dom'), may hold values from 0.5 to 2
- shear_modulus: float32 [64, 12288], P(None, 'dom'), may hold values from 0.5 to 2
- neighbour: int32 [6, 12288], P(None, 'dom'), may hold values from -1 to 1647, as said below
- send_list: int32 [2, 7040], P(None, 'dom'), may hold values from -1 to 4607, as said below
Outputs:
- adjoint_velocity: float32 [48, 3, 64, 12288], P('event', None, None, 'dom')
- kernels: float32 [3, 16, 49152], P(None, 'dom', 'event')
The draws below stay inside these ranges and needn't reach their ends.
Inputs may be any that keep to these rules, and one draw needn't show every extreme that they name: `neighbour`: codes 0 to 767 name a slot of the same block, and then that slot's face f xor 1 names this face back; a code 768 + j names position j of row 1 of block b - 1 in send_list, a code 768 + 440 + j position j of row 0 of block b + 1, and such a position holds the partner face; -1 marks outer faces and every face of an unused slot. Every used slot has at least one face with a code other than -1; the used slots of a block come first. In every draw some block uses all 768 slots. `send_list`: positions b * 440 to (b + 1) * 440 - 1 belong to block b: row 0 lists the faces of b whose partner lies in block b - 1, row 1 those whose partner lies in block b + 1, each as f * 768 + s, used positions first and -1 after them. In every draw some block fills all 440 positions of row 0 and some block all 440 of row 1.
All inputs are finite; a program needn't handle non-finite values.
Results may differ from the reference program's by a relative error of at most 0.0001.
Values sent between devices are 32-bit elements; how exact they have to be, the bound alone decides.
A program may use at most 128 MiB of HBM per device.

```python
import math
import jax
import jax.numpy as jnp
import numpy as np
from jax import lax

GY = 12
GZ = 8
SLAB = 6
SHIFT = 1
NODES = 64
STEPS = 3
E_DEV = 768
E_TOTAL = 12288
CAP = 440
EVENTS = 48
N_DOM = 16


def build_mesh(key):
    columns = GY * GZ
    extent = N_DOM * SLAB
    slot_count = E_DEV
    key_shift, key_chosen, key_pattern, key_order, key_phase = jax.random.split(key, 5)
    drawn_shift = jax.random.randint(key_shift, (N_DOM + 1, columns), -SHIFT, SHIFT + 1).astype(jnp.int32)
    block_ids = jnp.arange(N_DOM + 1, dtype=jnp.int32)[:, None]
    column_ids = jnp.arange(columns, dtype=jnp.int32)
    phase = jax.random.randint(key_phase, (), 0, 2).astype(jnp.int32) * 2 - 1
    checker = ((column_ids // GZ + column_ids % GZ) % 2 * 2 - 1) * phase
    chosen = jax.random.randint(key_chosen, (), 1, N_DOM - 1).astype(jnp.int32)
    patterned = jax.random.randint(key_pattern, (), 1, N_DOM - 2).astype(jnp.int32)
    patterned = jnp.where(patterned >= chosen, patterned + 2, patterned)
    cuts = block_ids * SLAB + drawn_shift
    cuts = jnp.where(block_ids == chosen, block_ids * SLAB - SHIFT, cuts)
    cuts = jnp.where(block_ids == chosen + 1, block_ids * SLAB + SHIFT, cuts)
    cuts = jnp.where(block_ids == patterned, block_ids * SLAB + SHIFT * checker[None, :], cuts)
    cuts = jnp.where(block_ids == 0, 0, cuts)
    cuts = jnp.where(block_ids == N_DOM, extent, cuts).astype(jnp.int32)
    thickness = cuts[1:] - cuts[:-1]
    column_order = jax.random.permutation(key_order, columns).astype(jnp.int32)
    ordered = thickness[:, column_order]
    ordered_starts = jnp.cumsum(ordered, axis=1) - ordered
    starts = jnp.zeros_like(thickness).at[:, column_order].set(ordered_starts)
    layer_ids = jnp.arange(extent, dtype=jnp.int32)[:, None]
    owner = jnp.sum((cuts[1:N_DOM][None, :, :] <= layer_ids[:, None, :]).astype(jnp.int32), axis=1)
    owner_cut = cuts[owner, column_ids[None, :]]
    slot_index = starts[owner, column_ids[None, :]] + layer_ids - owner_cut
    steps_x = jnp.array([-1, 1, 0, 0, 0, 0], jnp.int32)[:, None, None]
    steps_y = jnp.array([0, 0, -1, 1, 0, 0], jnp.int32)[:, None, None]
    steps_z = jnp.array([0, 0, 0, 0, -1, 1], jnp.int32)[:, None, None]
    near_x = layer_ids[None] + steps_x
    near_y = (column_ids // GZ)[None, None, :] + steps_y
    near_z = (column_ids % GZ)[None, None, :] + steps_z
    inside = (near_x >= 0) & (near_x < extent) & (near_y >= 0) & (near_y < GY) & (near_z >= 0) & (near_z < GZ)
    clip_x = jnp.clip(near_x, 0, extent - 1)
    near_column = jnp.clip(near_y, 0, GY - 1) * GZ + jnp.clip(near_z, 0, GZ - 1)
    full_shape = (6, extent, columns)
    near_owner = jnp.broadcast_to(owner[clip_x, near_column], full_shape)
    near_slot = jnp.broadcast_to(slot_index[clip_x, near_column], full_shape)
    inside = jnp.broadcast_to(inside, full_shape)
    own_owner = jnp.broadcast_to(owner[None], full_shape)
    own_slot = jnp.broadcast_to(slot_index[None], full_shape)
    face_ids = jnp.broadcast_to(jnp.arange(6, dtype=jnp.int32)[:, None, None], full_shape)
    to_lower = (inside & (near_owner == own_owner - 1)).astype(jnp.int32)
    to_upper = (inside & (near_owner == own_owner + 1)).astype(jnp.int32)
    face_key = face_ids * slot_count + own_slot
    lower_mark = jnp.zeros((N_DOM, 6 * slot_count), jnp.int32).at[own_owner, face_key].add(to_lower)
    upper_mark = jnp.zeros((N_DOM, 6 * slot_count), jnp.int32).at[own_owner, face_key].add(to_upper)
    lower_rank = jnp.cumsum(lower_mark, axis=1) - lower_mark
    upper_rank = jnp.cumsum(upper_mark, axis=1) - upper_mark
    mark_blocks = jnp.broadcast_to(jnp.arange(N_DOM, dtype=jnp.int32)[:, None], (N_DOM, 6 * slot_count))
    key_values = jnp.broadcast_to(jnp.arange(6 * slot_count, dtype=jnp.int32)[None, :], (N_DOM, 6 * slot_count))
    lower_target = jnp.where(lower_mark > 0, lower_rank, CAP)
    upper_target = jnp.where(upper_mark > 0, upper_rank, CAP)
    lower_list = jnp.full((N_DOM, CAP + 1), -1, jnp.int32).at[mark_blocks, lower_target].set(jnp.where(lower_mark > 0, key_values, -1))[:, :CAP]
    upper_list = jnp.full((N_DOM, CAP + 1), -1, jnp.int32).at[mark_blocks, upper_target].set(jnp.where(upper_mark > 0, key_values, -1))[:, :CAP]
    send_list = jnp.stack([lower_list.reshape(-1), upper_list.reshape(-1)])
    swapped_key = (face_ids ^ 1) * slot_count + near_slot
    code_lower = slot_count + upper_rank[near_owner, swapped_key]
    code_upper = slot_count + CAP + lower_rank[near_owner, swapped_key]
    code = jnp.where(near_owner == own_owner, near_slot, jnp.where(near_owner == own_owner - 1, code_lower, code_upper))
    code = jnp.where(inside, code, -1).astype(jnp.int32)
    neighbour = jnp.full((6, N_DOM * slot_count), -1, jnp.int32).at[face_ids, own_owner * slot_count + own_slot].set(code)
    return (neighbour, send_list)


def draw_neighbour(key, part):
    return build_mesh(jax.random.fold_in(key, 11))[0]


def draw_send_list(key, part):
    return build_mesh(jax.random.fold_in(key, 11))[1]


def shard_levels(rng, shape, cuts, smallest, largest):
    def one(dim, blocks):
        heights = jax.random.uniform(jax.random.fold_in(jax.random.fold_in(rng, 6), dim), (blocks,), jnp.float32, smallest / len(cuts), largest / len(cuts))
        return jnp.repeat(jnp.exp(heights), shape[dim] // blocks).reshape((-1,) + (1,) * (len(shape) - dim - 1))

    loudness = one(*cuts[0])
    for cut in cuts[1:]:
        loudness = loudness * one(*cut)
    return loudness


def scatter_about(rng, shape, scale, most, shards=(), kind=jnp.bfloat16):
    factor_of = shard_levels(rng, shape, shards, -0.22, 0.18) if shards else 1.0
    drawn = jax.random.normal(rng, shape, jnp.float32) * scale * factor_of
    return jnp.minimum(jnp.maximum(drawn, -most), most).astype(kind)


def setup_inputs(seed: int = 0) -> dict:
    arg_keys = jax.random.split(jax.random.key(seed), 8)
    adjoint_state = scatter_about(arg_keys[0], (EVENTS, 9, NODES, E_TOTAL), 1.0, 6.0, ((0, 48), (3, 16)), jnp.float32)
    forward_velocity = scatter_about(arg_keys[1], (EVENTS, STEPS, 3, NODES, E_TOTAL), 1.0, 6.0, ((0, 48), (4, 16)), jnp.float32)
    density = jnp.clip(jnp.exp(math.log(3.0) - 1.0986123 * jax.random.uniform(arg_keys[2], (NODES, E_TOTAL), jnp.float32) ** shard_levels(arg_keys[2], (NODES, E_TOTAL), ((1, 16),), -0.2, 0.2)), 1.0, 3.0)
    lame_lambda = jnp.clip(jnp.exp(math.log(2.0) - 1.3862944 * jax.random.uniform(arg_keys[3], (NODES, E_TOTAL), jnp.float32) ** shard_levels(arg_keys[3], (NODES, E_TOTAL), ((1, 16),), -0.2, 0.2)), 0.5, 2.0)
    shear_modulus = jnp.clip(jnp.exp(math.log(2.0) - 1.3862944 * jax.random.uniform(arg_keys[4], (NODES, E_TOTAL), jnp.float32) ** shard_levels(arg_keys[4], (NODES, E_TOTAL), ((1, 16),), -0.2, 0.2)), 0.5, 2.0)
    neighbour = draw_neighbour(jax.random.fold_in(arg_keys[7], 71), 0)
    send_list = draw_send_list(jax.random.fold_in(arg_keys[7], 71), 0)
    return dict(adjoint_state=adjoint_state, forward_velocity=forward_velocity, density=density, lame_lambda=lame_lambda, shear_modulus=shear_modulus, neighbour=neighbour, send_list=send_list)


time_step = 0.02
lift_weight = 6.0
component_pairs = ((0, 0), (1, 1), (2, 2), (0, 1), (0, 2), (1, 2))
symmetric_index = ((0, 3, 4), (3, 1, 5), (4, 5, 2))

def lobatto_diff():
    points = [-1.0, -1.0 / math.sqrt(5.0), 1.0 / math.sqrt(5.0), 1.0]
    weights = [1.0 / math.prod([points[target] - points[other] for other in range(4) if other != target]) for target in range(4)]
    offdiag = [[0.0 if target == source else weights[source] / weights[target] / (points[target] - points[source]) for source in range(4)] for target in range(4)]
    return np.array([[-sum(offdiag[target]) if target == source else offdiag[target][source] for source in range(4)] for target in range(4)], dtype=np.float32)

def face_table():
    entries = []
    for face_node in range(16):
        first_index = face_node // 4
        second_index = face_node % 4
        layout = []
        for face_id in range(6):
            coordinates = [first_index, second_index]
            coordinates.insert(face_id // 2, 3 * (face_id % 2))
            layout.append(16 * coordinates[0] + 4 * coordinates[1] + coordinates[2])
        entries.append(layout)
    return np.array(entries, dtype=np.int32)

def normal_table():
    return np.array([[face_id % 2 * 2 - 1.0 if face_id // 2 == direction else 0.0 for face_id in range(6)] for direction in range(3)], dtype=np.float32)

def lift_table():
    nodes_of = face_table()
    return np.array([[lift_weight if nodes_of[column // 6, column % 6] == node_id else 0.0 for column in range(96)] for node_id in range(64)], dtype=np.float32)

def normal_parts():
    normals = jnp.asarray(normal_table())
    return normals[:, None, :, None]

def lift_apply(face_terms):
    matrix = jnp.asarray(lift_table())
    components = face_terms.shape[0]
    return jnp.einsum('nm,cme->cne', matrix, face_terms.reshape(components, 96, face_terms.shape[-1]), precision=lax.Precision.HIGHEST)

def stress_faces(velocity_jump, lame_face, shear_face):
    shaped = normal_parts()
    along = velocity_jump[0] * shaped[0] + velocity_jump[1] * shaped[1] + velocity_jump[2] * shaped[2]
    pieces = []
    for first, second in component_pairs:
        shear_part = shear_face * (velocity_jump[first] * shaped[second] + velocity_jump[second] * shaped[first])
        if first == second:
            pieces.append(0.5 * (lame_face * along + shear_part))
        else:
            pieces.append(0.5 * shear_part)
    return jnp.stack(pieces)

def traction_of(traces):
    shaped = normal_parts()
    return jnp.stack([traces[symmetric_index[component][0]] * shaped[0] + traces[symmetric_index[component][1]] * shaped[1] + traces[symmetric_index[component][2]] * shaped[2] for component in range(3)])

def stress_rate(gradient, lame_first, shear_mod):
    trace_sum = gradient[0, 0] + gradient[1, 1] + gradient[2, 2]
    pieces = []
    for first, second in component_pairs:
        shear_part = shear_mod * (gradient[first, second] + gradient[second, first])
        if first == second:
            pieces.append(lame_first * trace_sum + shear_part)
        else:
            pieces.append(shear_part)
    return jnp.stack(pieces)

def divergence(stress_grad):
    return jnp.stack([stress_grad[symmetric_index[component][0], 0] + stress_grad[symmetric_index[component][1], 1] + stress_grad[symmetric_index[component][2], 2] for component in range(3)])

def kernel_terms(forward, velocity, stress, forward_grad):
    rho_term = -time_step * (forward[0] * velocity[0] + forward[1] * velocity[1] + forward[2] * velocity[2])
    trace_rate = forward_grad[0, 0] + forward_grad[1, 1] + forward_grad[2, 2]
    lame_term = -time_step * trace_rate * (stress[0] + stress[1] + stress[2])
    contraction = 0.0
    for first in range(3):
        for second in range(3):
            contraction = contraction + 0.5 * (forward_grad[first, second] + forward_grad[second, first]) * stress[symmetric_index[first][second]]
    shear_term = -time_step * 2.0 * contraction
    return jnp.stack([rho_term, lame_term, shear_term])

def volume_grad(nodal_field):
    components = nodal_field.shape[0]
    width = nodal_field.shape[-1]
    cube = nodal_field.reshape(components, 4, 4, 4, width)
    matrix = jnp.asarray(lobatto_diff())
    along_x = jnp.einsum('ai,cijke->cajke', matrix, cube, precision=lax.Precision.HIGHEST)
    along_y = jnp.einsum('aj,cijke->ciake', matrix, cube, precision=lax.Precision.HIGHEST)
    along_z = jnp.einsum('ak,cijke->cijae', matrix, cube, precision=lax.Precision.HIGHEST)
    return jnp.stack([along_x, along_y, along_z], 1).reshape(components, 3, 64, width)

def plus_values(traces, partner):
    trace_cols = traces.reshape(traces.shape[0] * 16, -1)
    return jnp.take(trace_cols, partner, axis=1).reshape(traces.shape)

def run_event(event_state, forward, partner, outer_sign, valid_mask, lame_first, shear_mod, density):
    nodes_of = face_table()
    lame_face = lame_first[nodes_of]
    shear_face = shear_mod[nodes_of]
    impedance = jnp.sqrt(density[nodes_of] * (lame_face + 2.0 * shear_face))
    velocity = event_state[0:3] * valid_mask
    stress = event_state[3:9] * valid_mask
    summed = jnp.zeros((3,) + density.shape, jnp.float32)
    for step in range(STEPS):
        vel_traces = velocity[:, nodes_of]
        velocity_jump = plus_values(vel_traces, partner) - vel_traces
        vel_grad = volume_grad(velocity)
        stress = stress + time_step * (stress_rate(vel_grad, lame_first, shear_mod) + lift_apply(stress_faces(velocity_jump, lame_face, shear_face)))
        str_traces = stress[:, nodes_of]
        plus_stress = plus_values(str_traces, partner) * outer_sign
        traction_jump = traction_of(plus_stress) - traction_of(str_traces)
        vel_faces = 0.5 * traction_jump + 0.5 * impedance * velocity_jump
        velocity = velocity + time_step / density * (divergence(volume_grad(stress)) + lift_apply(vel_faces))
        summed = summed + kernel_terms(forward[step], velocity, stress, volume_grad(forward[step]))
    return (velocity, summed)

def reference(adjoint_state, forward_velocity, density, lame_lambda, shear_modulus, neighbour, send_list):
    all_slots = density.shape[1]
    slot_count = all_slots // N_DOM
    capacity = send_list.shape[1] // N_DOM
    face_ids = lax.broadcasted_iota(jnp.int32, neighbour.shape, 0)
    global_ids = lax.broadcasted_iota(jnp.int32, neighbour.shape, 1)
    block_ids = global_ids // slot_count
    own_key = face_ids * all_slots + global_ids
    same_key = (face_ids ^ 1) * all_slots + block_ids * slot_count + neighbour
    lower_block = jnp.clip(block_ids - 1, 0, N_DOM - 1)
    upper_block = jnp.clip(block_ids + 1, 0, N_DOM - 1)
    lower_entry = send_list[1, lower_block * capacity + jnp.clip(neighbour - slot_count, 0, capacity - 1)]
    upper_entry = send_list[0, upper_block * capacity + jnp.clip(neighbour - slot_count - capacity, 0, capacity - 1)]
    lower_key = lower_entry // slot_count * all_slots + lower_block * slot_count + lower_entry % slot_count
    upper_key = upper_entry // slot_count * all_slots + upper_block * slot_count + upper_entry % slot_count
    partner = jnp.where(neighbour < 0, own_key, jnp.where(neighbour < slot_count, same_key, jnp.where(neighbour < slot_count + capacity, lower_key, upper_key))).reshape(-1)
    outer_sign = jnp.where(neighbour < 0, -1.0, 1.0).astype(jnp.float32)[None, None]
    valid_mask = jnp.any(neighbour >= 0, axis=0).astype(jnp.float32)

    def one_event(kernel_total, inputs):
        event_state, forward = inputs
        velocity, summed = run_event(event_state, forward, partner, outer_sign, valid_mask, lame_lambda, shear_modulus, density)
        return (kernel_total + summed, velocity)
    kernel_total, velocities = lax.scan(one_event, jnp.zeros((3, 64, all_slots), jnp.float32), (adjoint_state, forward_velocity))
    kernels = kernel_total.reshape(3, 64, N_DOM, slot_count).transpose(0, 2, 1, 3).reshape(3, N_DOM, 64 * slot_count)
    return (velocities, kernels)
```

```python
import functools
import math

import jax
import jax.numpy as jnp
import numpy as np
from jax import lax
from jax.experimental import pallas as pl
from jax.experimental.pallas import tpu as pltpu
from jax.sharding import PartitionSpec as P
import ml_dtypes

time_step = 0.02
half_lift = 3.0
symmetric_index = ((0, 3, 4), (3, 1, 5), (4, 5, 2))
SIDE = 512
MESH = pl.DeviceIdType.MESH
f32 = jnp.float32
bf16 = jnp.bfloat16


def lobatto_diff():
    points = [-1.0, -1.0 / math.sqrt(5.0), 1.0 / math.sqrt(5.0), 1.0]
    weights = [
        1.0 / math.prod([points[target] - points[other] for other in range(4) if other != target])
        for target in range(4)
    ]
    offdiag = [
        [
            (
                0.0
                if target == source
                else weights[source] / weights[target] / (points[target] - points[source])
            )
            for source in range(4)
        ]
        for target in range(4)
    ]
    return np.array(
        [
            [
                -sum(offdiag[target]) if target == source else offdiag[target][source]
                for source in range(4)
            ]
            for target in range(4)
        ],
        dtype=np.float32,
    )


def deriv_table():
    matrix = lobatto_diff()
    identity = np.eye(4, dtype=np.float32)
    return np.concatenate(
        [
            np.kron(np.kron(matrix, identity), identity),
            np.kron(np.kron(identity, matrix), identity),
            np.kron(np.kron(identity, identity), matrix),
        ],
        axis=0,
    ).astype(np.float32)


def face_nodes():
    nodes = np.zeros((6, 16), np.int32)
    for face in range(6):
        for q in range(16):
            coordinates = [q // 4, q % 4]
            coordinates.insert(face // 2, 3 * (face % 2))
            nodes[face, q] = 16 * coordinates[0] + 4 * coordinates[1] + coordinates[2]
    return nodes


def tables():
    to_bf16 = lambda x: np.asarray(x, np.float32).astype(ml_dtypes.bfloat16)
    deriv = deriv_table()
    high = to_bf16(deriv)
    low = to_bf16(deriv - high.astype(np.float32))
    deriv3 = np.concatenate([high, low, high], axis=1)
    nodes = face_nodes()
    extract = np.zeros((96, 64), np.float32)
    signed = np.zeros((192, 96), np.float32)
    summed = np.zeros((64, 96), np.float32)
    plain = np.zeros((64, 96), np.float32)
    for face in range(6):
        sign = face % 2 * 2 - 1.0
        for q in range(16):
            column, node = face * 16 + q, nodes[face, q]
            extract[column, node] = 1.0
            signed[face // 2 * 64 + node, column] = half_lift * sign
            summed[node, column] = half_lift * sign
            plain[node, column] = half_lift
    grad_rows = np.concatenate([deriv3.astype(np.float32), signed, signed], axis=1)
    jump_rows = np.concatenate([np.zeros((64, 192), np.float32), plain, plain], axis=1)
    stage_a = np.concatenate([grad_rows, jump_rows], axis=0)
    lift2 = np.concatenate([summed, summed], axis=1)
    return to_bf16(stage_a), deriv3, to_bf16(lift2), to_bf16(extract)


def split(x):
    high = x.astype(bf16)
    return high, (x - high.astype(f32)).astype(bf16)


def dot(a, b):
    return jnp.dot(a, b, preferred_element_type=f32)


def sim_kernel(
    state, forward, rho, lam, mu, near, sends, stage_a, deriv3, lift2, extract,
    vel, acc,
    sig, onehot, pick, send_ids, traces, jump, grad_in, grad, fgrad, sig_in, jump_in, impulse, div,
    halves, out_buf, in_buf, send_sem, recv_sem,
):
    count = lax.axis_size("dom")
    me = lax.axis_index("dom")
    lower = lax.rem(me + count - 1, count)
    upper = lax.rem(me + 1, count)
    slots = rho.shape[1]
    cap = sends.shape[1]
    top = slots + 2 * SIDE
    steps = forward.shape[1]

    barrier = pltpu.get_barrier_semaphore()
    for other in (lower, upper):
        pl.semaphore_signal(barrier, inc=1, device_id={"dom": other}, device_id_type=MESH)

    valid = jnp.where(jnp.max(near[...], axis=0, keepdims=True) >= 0, 1.0, 0.0)
    for c in range(3):
        vel[0, c] = state[0, c] * valid
    for c in range(6):
        sig[c] = state[0, 3 + c] * valid
    acc[...] = jnp.zeros_like(acc)

    send_ids[...] = jnp.full_like(send_ids, -1)
    send_ids[0:1, 0:cap] = sends[0:1, :]
    send_ids[0:1, SIDE : SIDE + cap] = sends[1:2, :]
    ids = send_ids[0:1, :]
    face_of = jnp.where(ids < 0, -1, 0)
    for f in range(1, 6):
        face_of = face_of + jnp.where(ids >= f * slots, 1, 0)
    slot_of = ids - face_of * slots
    slot_of = jnp.where(ids < 0, -1, slot_of)

    def build_pick(k, carry):
        rows = pl.ds(pl.multiple_of(k * 64, 64), 64)
        index = lax.broadcasted_iota(jnp.int32, (64, 2 * SIDE), 0) + k * 64
        pick[rows, :] = jnp.where(index == slot_of, 1.0, 0.0).astype(bf16)
        return carry

    lax.fori_loop(0, slots // 64, build_pick, 0)

    def inner_of(f):
        return jnp.where(near[f : f + 1, :] >= 0, 1.0, 0.0)

    def copies(phase):
        return [
            pltpu.make_async_remote_copy(
                src_ref=out_buf.at[phase, side],
                dst_ref=in_buf.at[phase, 1 - side],
                send_sem=send_sem.at[phase, side],
                recv_sem=recv_sem.at[phase, 1 - side],
                device_id={"dom": other},
                device_id_type=MESH,
            )
            for side, other in ((0, lower), (1, upper))
        ]

    def send(phase):
        rows = traces[...].reshape(576, slots)
        for side in range(2):
            for part in range(SIDE // 256):
                start = side * SIDE + part * 256
                got = dot(rows, pick[:, start : start + 256])
                face = face_of[:, start : start + 256]
                total = jnp.zeros((48, 256), f32)
                for f in range(6):
                    both = got[f * 96 : f * 96 + 48] + got[f * 96 + 48 : f * 96 + 96]
                    total = jnp.where(face == f, both, total)
                out_buf[phase, side, :, part * 256 : part * 256 + 256] = total
        for copy in copies(phase):
            copy.start()

    def own(phase):
        for f in range(6):
            got = dot(traces[f ^ 1], onehot[f, 0:slots, :])
            mine = traces[f, 0:48].astype(f32) + traces[f, 48:96].astype(f32)
            weight = inner_of(f) if phase == 0 else 2.0 - inner_of(f)
            jump[f] = got[0:48] + got[48:96] - mine * weight

    def arrive(phase, target, base):
        for copy in copies(phase):
            copy.wait()
        for side in range(2):
            high, low = split(in_buf[phase, side])
            halves[0:48, side * SIDE : side * SIDE + SIDE] = high
            halves[48:96, side * SIDE : side * SIDE + SIDE] = low
        for f in range(6):
            got = dot(halves[...], onehot[f, slots:top, :])
            high, low = split(jump[f] + got[0:48] + got[48:96])
            for c in range(3):
                target[c, base + f * 16 : base + f * 16 + 16] = high[c * 16 : c * 16 + 16]
                target[c, base + 96 + f * 16 : base + 112 + f * 16] = low[c * 16 : c * 16 + 16]

    def put3(ref, index, high, low):
        ref[index, 0:64] = high
        ref[index, 64:128] = high
        ref[index, 128:192] = low

    def velocity_traces():
        for c in range(3):
            high, low = split(vel[0, c])
            put3(grad_in, c, high, low)
            for part, x in enumerate((high, low)):
                got = dot(extract[...], x).astype(bf16)
                for f in range(6):
                    at = part * 48 + c * 16
                    traces[f, at : at + 16] = got[f * 16 : f * 16 + 16]

    def stress_traces():
        for m, pairs in enumerate(
            (((0, 0),), ((1, 1),), ((2, 2),), ((1, 0), (0, 1)), ((2, 0), (0, 2)), ((2, 1), (1, 2)))
        ):
            high, low = split(sig[m])
            put3(sig_in, m, high, low)
            for part, x in enumerate((high, low)):
                for c, d in pairs:
                    got = dot(extract[d * 32 : d * 32 + 32, :], x).astype(bf16)
                    for end in range(2):
                        at = part * 48 + c * 16
                        traces[2 * d + end, at : at + 16] = got[end * 16 : end * 16 + 16]

    def build_onehot():
        for f in range(6):
            code = near[f : f + 1, :]
            code = jnp.where(code >= slots + cap, code + (SIDE - cap), code)

            def body(k, carry):
                rows = pl.ds(pl.multiple_of(k * 64, 64), 64)
                index = lax.broadcasted_iota(jnp.int32, (64, slots), 0) + k * 64
                onehot[f, rows, :] = jnp.where(index == code, 1.0, 0.0).astype(bf16)
                return carry

            lax.fori_loop(0, top // 64, body, 0)

    def step(n, carry):
        velocity_traces()

        @pl.when(n == 0)
        def _():
            pl.semaphore_wait(barrier, 2)

        send(0)

        @pl.when(n == 0)
        def _():
            build_onehot()

        own(0)
        for c in range(3):
            high, low = split(forward[0, n, c])
            stack = jnp.concatenate([high, high, low], axis=0)
            fgrad[c] = dot(deriv3[...], stack)
        arrive(0, grad_in, 192)
        for c in range(3):
            grad[c] = dot(stage_a[...], grad_in[c])
        for r in range(0, 64, 16):
            rows = slice(r, r + 16)
            g = [[grad[i, j * 64 + r : j * 64 + r + 16] for j in range(3)] for i in range(3)]
            shear = mu[rows] * time_step
            bulk = lam[rows] * time_step * (g[0][0] + g[1][1] + g[2][2])
            for c in range(3):
                sig[c, rows] = sig[c, rows] + (bulk + 2.0 * shear * g[c][c])
            for m, (i, j) in ((3, (0, 1)), (4, (0, 2)), (5, (1, 2))):
                sig[m, rows] = sig[m, rows] + shear * (g[i][j] + g[j][i])
        stress_traces()
        send(1)
        own(1)
        for c in range(3):
            total = dot(deriv3[0:64], sig_in[symmetric_index[c][0]])
            total = total + dot(deriv3[64:128], sig_in[symmetric_index[c][1]])
            total = total + dot(deriv3[128:192], sig_in[symmetric_index[c][2]])
            div[c] = total
        for r in range(0, 64, 16):
            rows = slice(r, r + 16)
            g = [[fgrad[i, j * 64 + r : j * 64 + r + 16] for j in range(3)] for i in range(3)]
            s = [sig[m, rows] for m in range(6)]
            rate = g[0][0] + g[1][1] + g[2][2]
            acc[1, rows] = acc[1, rows] - time_step * rate * (s[0] + s[1] + s[2])
            contraction = g[0][0] * s[0] + g[1][1] * s[1] + g[2][2] * s[2]
            contraction = contraction + (g[0][1] + g[1][0]) * s[3]
            contraction = contraction + (g[0][2] + g[2][0]) * s[4]
            contraction = contraction + (g[1][2] + g[2][1]) * s[5]
            acc[2, rows] = acc[2, rows] - (2.0 * time_step) * contraction
        arrive(1, jump_in, 0)
        for c in range(3):
            impulse[c] = dot(lift2[...], jump_in[c])
        for r in range(0, 64, 16):
            rows = slice(r, r + 16)
            z = jnp.sqrt(rho[rows] * (lam[rows] + 2.0 * mu[rows]))
            scale = time_step / rho[rows]
            total = jnp.zeros_like(z)
            for c in range(3):
                rate = div[c, rows] + impulse[c, rows] + z * grad[c, 192 + r : 192 + r + 16]
                new = vel[0, c, rows] + scale * rate
                vel[0, c, rows] = new
                total = total + forward[0, n, c, rows] * new
            acc[0, rows] = acc[0, rows] - time_step * total
        return carry

    lax.fori_loop(0, steps, step, 0)


def local(
    adjoint_state, forward_velocity, density, lame_lambda, shear_modulus, neighbour, send_list
):
    slots = density.shape[1]
    top = slots + 2 * SIDE
    stage_a, deriv3, lift2, extract = (jnp.asarray(x) for x in tables())
    vmem = pl.BlockSpec(memory_space=pltpu.VMEM)
    velocity, terms = pl.pallas_call(
        sim_kernel,
        out_shape=(
            jax.ShapeDtypeStruct((1, 3, 64, slots), f32),
            jax.ShapeDtypeStruct((3, 64, slots), f32),
        ),
        in_specs=[vmem] * 11,
        out_specs=(vmem, vmem),
        scratch_shapes=[
            pltpu.VMEM((6, 64, slots), f32),
            pltpu.VMEM((6, top, slots), bf16),
            pltpu.VMEM((slots, 2 * SIDE), bf16),
            pltpu.VMEM((8, 2 * SIDE), jnp.int32),
            pltpu.VMEM((6, 96, slots), bf16),
            pltpu.VMEM((6, 48, slots), f32),
            pltpu.VMEM((3, 384, slots), bf16),
            pltpu.VMEM((3, 256, slots), f32),
            pltpu.VMEM((3, 192, slots), f32),
            pltpu.VMEM((6, 192, slots), bf16),
            pltpu.VMEM((3, 192, slots), bf16),
            pltpu.VMEM((3, 64, slots), f32),
            pltpu.VMEM((3, 64, slots), f32),
            pltpu.VMEM((96, 2 * SIDE), bf16),
            pltpu.VMEM((2, 2, 48, SIDE), f32),
            pltpu.VMEM((2, 2, 48, SIDE), f32),
            pltpu.SemaphoreType.DMA((2, 2)),
            pltpu.SemaphoreType.DMA((2, 2)),
        ],
        compiler_params=pltpu.CompilerParams(
            collective_id=0, has_side_effects=True, vmem_limit_bytes=60 * 1024 * 1024
        ),
    )(
        adjoint_state, forward_velocity, density, lame_lambda, shear_modulus, neighbour, send_list,
        stage_a, deriv3, lift2, extract,
    )
    part = lax.psum_scatter(terms.reshape(3, -1), "event", scatter_dimension=1, tiled=True)
    return (velocity, part.reshape(3, 1, -1))


def solution(mesh):
    placed = (
        P("event", None, None, "dom"),
        P("event", None, None, None, "dom"),
        P(None, "dom"),
        P(None, "dom"),
        P(None, "dom"),
        P(None, "dom"),
        P(None, "dom"),
    )
    return jax.shard_map(
        local,
        mesh=mesh,
        in_specs=placed,
        out_specs=(P("event", None, None, "dom"), P(None, "dom", "event")),
        check_vma=False,
    )
```

```python
import functools
import math

import jax
import jax.numpy as jnp
import numpy as np
from jax import lax
from jax.experimental import pallas as pl
from jax.experimental.pallas import tpu as pltpu
from jax.sharding import PartitionSpec as P
import ml_dtypes

time_step = 0.02
half_lift = 3.0
symmetric_index = ((0, 3, 4), (3, 1, 5), (4, 5, 2))
SIDE = 512
NX, NZ = 4, 12
MESH = pl.DeviceIdType.MESH
f32 = jnp.float32
bf16 = jnp.bfloat16


def lobatto_diff():
    points = [-1.0, -1.0 / math.sqrt(5.0), 1.0 / math.sqrt(5.0), 1.0]
    weights = [
        1.0 / math.prod([points[target] - points[other] for other in range(4) if other != target])
        for target in range(4)
    ]
    offdiag = [
        [
            (
                0.0
                if target == source
                else weights[source] / weights[target] / (points[target] - points[source])
            )
            for source in range(4)
        ]
        for target in range(4)
    ]
    return np.array(
        [
            [
                -sum(offdiag[target]) if target == source else offdiag[target][source]
                for source in range(4)
            ]
            for target in range(4)
        ],
        dtype=np.float32,
    )


def deriv_table():
    matrix = lobatto_diff()
    identity = np.eye(4, dtype=np.float32)
    return np.concatenate(
        [
            np.kron(np.kron(matrix, identity), identity),
            np.kron(np.kron(identity, matrix), identity),
            np.kron(np.kron(identity, identity), matrix),
        ],
        axis=0,
    ).astype(np.float32)


def face_nodes():
    nodes = np.zeros((6, 16), np.int32)
    for face in range(6):
        for q in range(16):
            coordinates = [q // 4, q % 4]
            coordinates.insert(face // 2, 3 * (face % 2))
            nodes[face, q] = 16 * coordinates[0] + 4 * coordinates[1] + coordinates[2]
    return nodes


def tables():
    to_bf16 = lambda x: np.asarray(x, np.float32).astype(ml_dtypes.bfloat16)
    deriv = deriv_table()
    high = to_bf16(deriv)
    low = to_bf16(deriv - high.astype(np.float32))
    deriv3 = np.concatenate([high, low, high], axis=1)
    nodes = face_nodes()
    extract = np.zeros((96, 64), np.float32)
    signed = np.zeros((192, 96), np.float32)
    summed = np.zeros((64, 96), np.float32)
    plain = np.zeros((64, 96), np.float32)
    for face in range(6):
        sign = face % 2 * 2 - 1.0
        for q in range(16):
            column, node = face * 16 + q, nodes[face, q]
            extract[column, node] = 1.0
            signed[face // 2 * 64 + node, column] = half_lift * sign
            summed[node, column] = half_lift * sign
            plain[node, column] = half_lift
    grad_rows = np.concatenate([deriv3.astype(np.float32), signed, signed], axis=1)
    jump_rows = np.concatenate([np.zeros((64, 192), np.float32), plain, plain], axis=1)
    stage_a = np.concatenate([grad_rows, jump_rows], axis=0)
    lift2 = np.concatenate([summed, summed], axis=1)
    return to_bf16(stage_a), deriv3, to_bf16(lift2), to_bf16(extract)


def split(x):
    high = x.astype(bf16)
    return high, (x - high.astype(f32)).astype(bf16)


def dot(a, b):
    return jnp.dot(a, b, preferred_element_type=f32)


def sim_kernel(
    state, forward, rho, lam, mu, near, sends, stage_a, deriv3, lift2, extract,
    vel, part,
    acc, sig, onehot, pick, send_ids, traces, jump, grad_in, grad, fgrad, sig_in, jump_in, impulse, div,
    halves, out_buf, in_buf, x_in, x_sum, z_out, z_in,
    send_sem, recv_sem, x_send, x_recv, z_send, z_recv,
):
    count = lax.axis_size("dom")
    me = lax.axis_index("dom")
    lower = lax.rem(me + count - 1, count)
    upper = lax.rem(me + 1, count)
    slots = rho.shape[1]
    cap = sends.shape[1]
    top = slots + 2 * SIDE
    steps = forward.shape[1]

    barrier = pltpu.get_barrier_semaphore()
    for other in (lower, upper):
        pl.semaphore_signal(barrier, inc=1, device_id={"dom": other}, device_id_type=MESH)
    event = lax.axis_index("event")
    along_x, along_z = event // NZ, lax.rem(event, NZ)
    x_peers = [lax.rem(along_x + d, NX) for d in range(1, NX)]
    z_peers = [lax.rem(along_z + d, NZ) for d in range(1, NZ)]
    peers = [p * NZ + along_z for p in x_peers] + [along_x * NZ + p for p in z_peers]
    for other in peers:
        pl.semaphore_signal(barrier, inc=1, device_id={"event": other}, device_id_type=MESH)
    band = 64 // NX

    def x_copies(group):
        terms = slice(1, 3) if group == 0 else slice(0, 1)
        return [
            pltpu.make_async_remote_copy(
                src_ref=acc.at[terms, pl.ds(pl.multiple_of(p * band, band), band), :],
                dst_ref=x_in.at[d, terms],
                send_sem=x_send.at[group, d],
                recv_sem=x_recv.at[group, d],
                device_id={"event": p * NZ + along_z},
                device_id_type=MESH,
            )
            for d, p in enumerate(x_peers)
        ]

    def z_copies(group):
        terms = slice(1, 3) if group == 0 else slice(0, 1)
        return [
            pltpu.make_async_remote_copy(
                src_ref=z_out.at[p, terms],
                dst_ref=z_in.at[d, terms],
                send_sem=z_send.at[group, d],
                recv_sem=z_recv.at[group, d],
                device_id={"event": along_x * NZ + p},
                device_id_type=MESH,
            )
            for d, p in enumerate(z_peers)
        ]

    def scatter_on(group):
        for copy in x_copies(group):
            copy.wait()
        mine = pl.ds(pl.multiple_of(along_x * band, band), band)
        for t in (1, 2) if group == 0 else (0,):
            total = acc[t, mine, :]
            for d in range(NX - 1):
                total = total + x_in[d, t]
            x_sum[t] = total
            for piece in range(band * slots // 128):
                row, column = piece // (slots // 128), piece % (slots // 128) * 128
                z_out[piece // 8, t, piece % 8 : piece % 8 + 1, :] = x_sum[t, row : row + 1, column : column + 128]
        for copy in z_copies(group):
            copy.start()

    def gather_in(group):
        for copy in z_copies(group):
            copy.wait()
        for t in (1, 2) if group == 0 else (0,):
            total = z_out[along_z, t]
            for d in range(NZ - 1):
                total = total + z_in[d, t]
            part[t] = total

    valid = jnp.where(jnp.max(near[...], axis=0, keepdims=True) >= 0, 1.0, 0.0)
    for c in range(3):
        vel[0, c] = state[0, c] * valid
    for c in range(6):
        sig[c] = state[0, 3 + c] * valid
    acc[...] = jnp.zeros_like(acc)

    send_ids[...] = jnp.full_like(send_ids, -1)
    send_ids[0:1, 0:cap] = sends[0:1, :]
    send_ids[0:1, SIDE : SIDE + cap] = sends[1:2, :]
    ids = send_ids[0:1, :]
    face_of = jnp.where(ids < 0, -1, 0)
    for f in range(1, 6):
        face_of = face_of + jnp.where(ids >= f * slots, 1, 0)
    slot_of = ids - face_of * slots
    slot_of = jnp.where(ids < 0, -1, slot_of)

    def build_pick(k, carry):
        rows = pl.ds(pl.multiple_of(k * 64, 64), 64)
        index = lax.broadcasted_iota(jnp.int32, (64, 2 * SIDE), 0) + k * 64
        pick[rows, :] = jnp.where(index == slot_of, 1.0, 0.0).astype(bf16)
        return carry

    lax.fori_loop(0, slots // 64, build_pick, 0)

    def inner_of(f):
        return jnp.where(near[f : f + 1, :] >= 0, 1.0, 0.0)

    def copies(phase):
        return [
            pltpu.make_async_remote_copy(
                src_ref=out_buf.at[phase, side],
                dst_ref=in_buf.at[phase, 1 - side],
                send_sem=send_sem.at[phase, side],
                recv_sem=recv_sem.at[phase, 1 - side],
                device_id={"dom": other},
                device_id_type=MESH,
            )
            for side, other in ((0, lower), (1, upper))
        ]

    def send(phase):
        rows = traces[...].reshape(576, slots)
        for side in range(2):
            for part in range(SIDE // 256):
                start = side * SIDE + part * 256
                got = dot(rows, pick[:, start : start + 256])
                face = face_of[:, start : start + 256]
                total = jnp.zeros((48, 256), f32)
                for f in range(6):
                    both = got[f * 96 : f * 96 + 48] + got[f * 96 + 48 : f * 96 + 96]
                    total = jnp.where(face == f, both, total)
                out_buf[phase, side, :, part * 256 : part * 256 + 256] = total
        for copy in copies(phase):
            copy.start()

    def own(phase):
        for f in range(6):
            got = dot(traces[f ^ 1], onehot[f, 0:slots, :])
            mine = traces[f, 0:48].astype(f32) + traces[f, 48:96].astype(f32)
            weight = inner_of(f) if phase == 0 else 2.0 - inner_of(f)
            jump[f] = got[0:48] + got[48:96] - mine * weight

    def arrive(phase, target, base):
        for copy in copies(phase):
            copy.wait()
        for side in range(2):
            high, low = split(in_buf[phase, side])
            halves[0:48, side * SIDE : side * SIDE + SIDE] = high
            halves[48:96, side * SIDE : side * SIDE + SIDE] = low
        for f in range(6):
            got = dot(halves[...], onehot[f, slots:top, :])
            high, low = split(jump[f] + got[0:48] + got[48:96])
            for c in range(3):
                target[c, base + f * 16 : base + f * 16 + 16] = high[c * 16 : c * 16 + 16]
                target[c, base + 96 + f * 16 : base + 112 + f * 16] = low[c * 16 : c * 16 + 16]

    def put3(ref, index, high, low):
        ref[index, 0:64] = high
        ref[index, 64:128] = high
        ref[index, 128:192] = low

    def velocity_traces():
        for c in range(3):
            high, low = split(vel[0, c])
            put3(grad_in, c, high, low)
            for part, x in enumerate((high, low)):
                got = dot(extract[...], x).astype(bf16)
                for f in range(6):
                    at = part * 48 + c * 16
                    traces[f, at : at + 16] = got[f * 16 : f * 16 + 16]

    def stress_traces():
        for m, pairs in enumerate(
            (((0, 0),), ((1, 1),), ((2, 2),), ((1, 0), (0, 1)), ((2, 0), (0, 2)), ((2, 1), (1, 2)))
        ):
            high, low = split(sig[m])
            put3(sig_in, m, high, low)
            for part, x in enumerate((high, low)):
                for c, d in pairs:
                    got = dot(extract[d * 32 : d * 32 + 32, :], x).astype(bf16)
                    for end in range(2):
                        at = part * 48 + c * 16
                        traces[2 * d + end, at : at + 16] = got[end * 16 : end * 16 + 16]

    def build_onehot():
        for f in range(6):
            code = near[f : f + 1, :]
            code = jnp.where(code >= slots + cap, code + (SIDE - cap), code)

            def body(k, carry):
                rows = pl.ds(pl.multiple_of(k * 64, 64), 64)
                index = lax.broadcasted_iota(jnp.int32, (64, slots), 0) + k * 64
                onehot[f, rows, :] = jnp.where(index == code, 1.0, 0.0).astype(bf16)
                return carry

            lax.fori_loop(0, top // 64, body, 0)

    def step(n, carry):
        velocity_traces()

        @pl.when(n == 0)
        def _():
            pl.semaphore_wait(barrier, 2 + len(peers))

        send(0)

        @pl.when(n == 0)
        def _():
            build_onehot()

        own(0)
        for c in range(3):
            high, low = split(forward[0, n, c])
            stack = jnp.concatenate([high, high, low], axis=0)
            fgrad[c] = dot(deriv3[...], stack)
        arrive(0, grad_in, 192)
        for c in range(3):
            grad[c] = dot(stage_a[...], grad_in[c])
        for r in range(0, 64, 16):
            rows = slice(r, r + 16)
            g = [[grad[i, j * 64 + r : j * 64 + r + 16] for j in range(3)] for i in range(3)]
            shear = mu[rows] * time_step
            bulk = lam[rows] * time_step * (g[0][0] + g[1][1] + g[2][2])
            for c in range(3):
                sig[c, rows] = sig[c, rows] + (bulk + 2.0 * shear * g[c][c])
            for m, (i, j) in ((3, (0, 1)), (4, (0, 2)), (5, (1, 2))):
                sig[m, rows] = sig[m, rows] + shear * (g[i][j] + g[j][i])
        stress_traces()
        send(1)
        own(1)
        for c in range(3):
            total = dot(deriv3[0:64], sig_in[symmetric_index[c][0]])
            total = total + dot(deriv3[64:128], sig_in[symmetric_index[c][1]])
            total = total + dot(deriv3[128:192], sig_in[symmetric_index[c][2]])
            div[c] = total
        for r in range(0, 64, 16):
            rows = slice(r, r + 16)
            g = [[fgrad[i, j * 64 + r : j * 64 + r + 16] for j in range(3)] for i in range(3)]
            s = [sig[m, rows] for m in range(6)]
            rate = g[0][0] + g[1][1] + g[2][2]
            acc[1, rows] = acc[1, rows] - time_step * rate * (s[0] + s[1] + s[2])
            contraction = g[0][0] * s[0] + g[1][1] * s[1] + g[2][2] * s[2]
            contraction = contraction + (g[0][1] + g[1][0]) * s[3]
            contraction = contraction + (g[0][2] + g[2][0]) * s[4]
            contraction = contraction + (g[1][2] + g[2][1]) * s[5]
            acc[2, rows] = acc[2, rows] - (2.0 * time_step) * contraction

        @pl.when(n == steps - 1)
        def _():
            for copy in x_copies(0):
                copy.start()

        arrive(1, jump_in, 0)
        for c in range(3):
            impulse[c] = dot(lift2[...], jump_in[c])
        for r in range(0, 64, 16):
            rows = slice(r, r + 16)
            z = jnp.sqrt(rho[rows] * (lam[rows] + 2.0 * mu[rows]))
            scale = time_step / rho[rows]
            total = jnp.zeros_like(z)
            for c in range(3):
                rate = div[c, rows] + impulse[c, rows] + z * grad[c, 192 + r : 192 + r + 16]
                new = vel[0, c, rows] + scale * rate
                vel[0, c, rows] = new
                total = total + forward[0, n, c, rows] * new
            acc[0, rows] = acc[0, rows] - time_step * total
        return carry

    lax.fori_loop(0, steps, step, 0)
    for copy in x_copies(1):
        copy.start()
    scatter_on(0)
    scatter_on(1)
    gather_in(0)
    gather_in(1)


def local(
    adjoint_state, forward_velocity, density, lame_lambda, shear_modulus, neighbour, send_list
):
    slots = density.shape[1]
    top = slots + 2 * SIDE
    stage_a, deriv3, lift2, extract = (jnp.asarray(x) for x in tables())
    vmem = pl.BlockSpec(memory_space=pltpu.VMEM)
    share = 64 * slots // (NX * NZ)
    velocity, part = pl.pallas_call(
        sim_kernel,
        out_shape=(
            jax.ShapeDtypeStruct((1, 3, 64, slots), f32),
            jax.ShapeDtypeStruct((3, share // 128, 128), f32),
        ),
        in_specs=[vmem] * 11,
        out_specs=(vmem, vmem),
        scratch_shapes=[
            pltpu.VMEM((3, 64, slots), f32),
            pltpu.VMEM((6, 64, slots), f32),
            pltpu.VMEM((6, top, slots), bf16),
            pltpu.VMEM((slots, 2 * SIDE), bf16),
            pltpu.VMEM((8, 2 * SIDE), jnp.int32),
            pltpu.VMEM((6, 96, slots), bf16),
            pltpu.VMEM((6, 48, slots), f32),
            pltpu.VMEM((3, 384, slots), bf16),
            pltpu.VMEM((3, 256, slots), f32),
            pltpu.VMEM((3, 192, slots), f32),
            pltpu.VMEM((6, 192, slots), bf16),
            pltpu.VMEM((3, 192, slots), bf16),
            pltpu.VMEM((3, 64, slots), f32),
            pltpu.VMEM((3, 64, slots), f32),
            pltpu.VMEM((96, 2 * SIDE), bf16),
            pltpu.VMEM((2, 2, 48, SIDE), f32),
            pltpu.VMEM((2, 2, 48, SIDE), f32),
            pltpu.VMEM((NX - 1, 3, 64 // NX, slots), f32),
            pltpu.VMEM((3, 64 // NX, slots), f32),
            pltpu.VMEM((NZ, 3, share // 128, 128), f32),
            pltpu.VMEM((NZ - 1, 3, share // 128, 128), f32),
            pltpu.SemaphoreType.DMA((2, 2)),
            pltpu.SemaphoreType.DMA((2, 2)),
            pltpu.SemaphoreType.DMA((2, NX - 1)),
            pltpu.SemaphoreType.DMA((2, NX - 1)),
            pltpu.SemaphoreType.DMA((2, NZ - 1)),
            pltpu.SemaphoreType.DMA((2, NZ - 1)),
        ],
        compiler_params=pltpu.CompilerParams(
            collective_id=0, has_side_effects=True, vmem_limit_bytes=60 * 1024 * 1024
        ),
    )(
        adjoint_state, forward_velocity, density, lame_lambda, shear_modulus, neighbour, send_list,
        stage_a, deriv3, lift2, extract,
    )
    return (velocity, part.reshape(3, 1, -1))


def solution(mesh):
    placed = (
        P("event", None, None, "dom"),
        P("event", None, None, None, "dom"),
        P(None, "dom"),
        P(None, "dom"),
        P(None, "dom"),
        P(None, "dom"),
        P(None, "dom"),
    )
    return jax.shard_map(
        local,
        mesh=mesh,
        in_specs=placed,
        out_specs=(P("event", None, None, "dom"), P(None, "dom", "event")),
        check_vma=False,
    )
```

```python
import functools
import math

import jax
import jax.numpy as jnp
import numpy as np
from jax import lax
from jax.experimental import pallas as pl
from jax.experimental.pallas import tpu as pltpu
from jax.sharding import PartitionSpec as P
import ml_dtypes

time_step = 0.02
half_lift = 3.0
symmetric_index = ((0, 3, 4), (3, 1, 5), (4, 5, 2))
SIDE = 512
HALF = 384
NX, NZ = 4, 12
SUM_EVENTS = True
MESH = pl.DeviceIdType.MESH
f32 = jnp.float32
bf16 = jnp.bfloat16


def lobatto_diff():
    points = [-1.0, -1.0 / math.sqrt(5.0), 1.0 / math.sqrt(5.0), 1.0]
    weights = [
        1.0 / math.prod([points[target] - points[other] for other in range(4) if other != target])
        for target in range(4)
    ]
    offdiag = [
        [
            (
                0.0
                if target == source
                else weights[source] / weights[target] / (points[target] - points[source])
            )
            for source in range(4)
        ]
        for target in range(4)
    ]
    return np.array(
        [
            [
                -sum(offdiag[target]) if target == source else offdiag[target][source]
                for source in range(4)
            ]
            for target in range(4)
        ],
        dtype=np.float32,
    )


def deriv_table():
    matrix = lobatto_diff()
    identity = np.eye(4, dtype=np.float32)
    return np.concatenate(
        [
            np.kron(np.kron(matrix, identity), identity),
            np.kron(np.kron(identity, matrix), identity),
            np.kron(np.kron(identity, identity), matrix),
        ],
        axis=0,
    ).astype(np.float32)


def face_nodes():
    nodes = np.zeros((6, 16), np.int32)
    for face in range(6):
        for q in range(16):
            coordinates = [q // 4, q % 4]
            coordinates.insert(face // 2, 3 * (face % 2))
            nodes[face, q] = 16 * coordinates[0] + 4 * coordinates[1] + coordinates[2]
    return nodes


def tables():
    to_bf16 = lambda x: np.asarray(x, np.float32).astype(ml_dtypes.bfloat16)
    deriv = deriv_table()
    high = to_bf16(deriv)
    low = to_bf16(deriv - high.astype(np.float32))
    deriv3 = np.concatenate([high, low, high], axis=1)
    nodes = face_nodes()
    signed = np.zeros((192, 96), np.float32)
    summed = np.zeros((64, 96), np.float32)
    plain = np.zeros((64, 96), np.float32)
    for face in range(6):
        sign = face % 2 * 2 - 1.0
        for q in range(16):
            column, node = face * 16 + q, nodes[face, q]
            signed[face // 2 * 64 + node, column] = half_lift * sign
            summed[node, column] = half_lift * sign
            plain[node, column] = half_lift
    stage_j = np.concatenate([signed, plain], axis=0)
    stage_j = np.concatenate([stage_j, stage_j], axis=1)
    lift2 = np.concatenate([summed, summed], axis=1)
    return deriv3, to_bf16(stage_j), to_bf16(lift2)


def split(x):
    high = x.astype(bf16)
    return high, (x - high.astype(f32)).astype(bf16)


def face_rows(tiles, dim):
    if dim == 0:
        return tiles[0:2], tiles[6:8]
    sub = lax.broadcasted_iota(jnp.int32, tiles[0].shape, 0)
    roll = lambda x, by: pltpu.roll(x, by % 8, 0) if by % 8 else x
    if dim == 1:
        low = [jnp.where(sub < 4, tiles[k], roll(tiles[k + 2], 4)) for k in (0, 4)]
        high = [jnp.where(sub < 4, roll(tiles[k + 1], 4), tiles[k + 3]) for k in (0, 4)]
        return low, high
    out = []
    for start in (0, 3):
        rows = []
        for k in (0, 4):
            total = roll(tiles[k], -start)
            for q in range(1, 8):
                total = jnp.where(sub == q, roll(tiles[k + q // 2], q - start - q % 2 * 4), total)
            rows.append(total)
        out.append(rows)
    return out


def dot(a, b):
    return jnp.dot(a, b, preferred_element_type=f32)


def sim_kernel(
    state, forward_hbm, rho, lam, mu, near, sends, stage_v, stage_j, lift2,
    vel_hbm, part,
    vel, forward, acc, sig, onehot, pick, spread, own_tile, own_hit, side_tile, side_hit, send_ids,
    traces, jump, field_in, jump_in, grad, kick, fgrad, sig_in, impulse, div, halves, face_at,
    out_buf, in_buf, x_in, x_sum, z_out, z_in,
    load_sem, send_sem, recv_sem, x_send, x_recv, z_send, z_recv,
):
    count = lax.axis_size("dom")
    me = lax.axis_index("dom")
    lower = lax.rem(me + count - 1, count)
    upper = lax.rem(me + 1, count)
    slots = rho.shape[1]
    cap = sends.shape[1]
    steps = forward.shape[0]

    load_v = pltpu.make_async_copy(state.at[0, 0:3], vel, load_sem.at[0])
    load_s = pltpu.make_async_copy(state.at[0, 3:9], sig, load_sem.at[1])
    load_f = pltpu.make_async_copy(forward_hbm.at[0], forward, load_sem.at[2])
    load_v.start()
    load_s.start()
    load_f.start()

    barrier = pltpu.get_barrier_semaphore()
    for other in (lower, upper):
        pl.semaphore_signal(barrier, inc=1, device_id={"dom": other}, device_id_type=MESH)
    event = lax.axis_index("event")
    along_x, along_z = event // NZ, lax.rem(event, NZ)
    x_peers = [lax.rem(along_x + d, NX) for d in range(1, NX)]
    z_peers = [lax.rem(along_z + d, NZ) for d in range(1, NZ)]
    peers = [p * NZ + along_z for p in x_peers] + [along_x * NZ + p for p in z_peers]
    if not SUM_EVENTS:
        peers = []
    for other in peers:
        pl.semaphore_signal(barrier, inc=1, device_id={"event": other}, device_id_type=MESH)
    band = 64 // NX

    def x_copies(group):
        terms = slice(1, 3) if group == 0 else slice(0, 1)
        return [
            pltpu.make_async_remote_copy(
                src_ref=acc.at[terms, pl.ds(pl.multiple_of(p * band, band), band), :],
                dst_ref=x_in.at[d, terms],
                send_sem=x_send.at[group, d],
                recv_sem=x_recv.at[group, d],
                device_id={"event": p * NZ + along_z},
                device_id_type=MESH,
            )
            for d, p in enumerate(x_peers)
        ]

    def z_copies(group):
        terms = slice(1, 3) if group == 0 else slice(0, 1)
        return [
            pltpu.make_async_remote_copy(
                src_ref=z_out.at[p, terms],
                dst_ref=z_in.at[d, terms],
                send_sem=z_send.at[group, d],
                recv_sem=z_recv.at[group, d],
                device_id={"event": along_x * NZ + p},
                device_id_type=MESH,
            )
            for d, p in enumerate(z_peers)
        ]

    def scatter_on(group):
        for copy in x_copies(group):
            copy.wait()
        mine = pl.ds(pl.multiple_of(along_x * band, band), band)
        for t in (1, 2) if group == 0 else (0,):
            total = acc[t, mine, :]
            for d in range(NX - 1):
                total = total + x_in[d, t]
            x_sum[t] = total
            for piece in range(band * slots // 128):
                row, column = piece // (slots // 128), piece % (slots // 128) * 128
                z_out[piece // 8, t, piece % 8 : piece % 8 + 1, :] = x_sum[t, row : row + 1, column : column + 128]
        for copy in z_copies(group):
            copy.start()

    def gather_in(group):
        for copy in z_copies(group):
            copy.wait()
        for t in (1, 2) if group == 0 else (0,):
            total = z_out[along_z, t]
            for d in range(NZ - 1):
                total = total + z_in[d, t]
            for row in range(8):
                part[t, :, row * 128 : row * 128 + 128] = total[row : row + 1, :]

    acc[...] = jnp.zeros_like(acc)

    send_ids[...] = jnp.full_like(send_ids, -1)
    send_ids[0:1, 0:cap] = sends[0:1, :]
    send_ids[0:1, SIDE : SIDE + cap] = sends[1:2, :]
    ids = send_ids[0:1, :]
    face_of = jnp.where(ids < 0, -1, 0)
    for f in range(1, 6):
        face_of = face_of + jnp.where(ids >= f * slots, 1, 0)
    slot_of = jnp.where(ids < 0, -1, ids - face_of * slots)

    def tile_of(index):
        width = index.shape[1]
        tile = jnp.right_shift(index, 4)
        row = lax.broadcasted_iota(jnp.int32, (16, width), 0)
        hit = jnp.where(jnp.bitwise_and(index, 15) == row, 1.0, 0.0)
        return jnp.broadcast_to(tile.astype(f32), (16, width)).astype(bf16), hit.astype(bf16)

    spread[0], spread[1] = tile_of(slot_of)

    def build_pick(k, carry):
        rows = pl.ds(pl.multiple_of(k * 16, 16), 16)
        level = jnp.full((16, 2 * SIDE), k.astype(f32)).astype(bf16)
        pick[rows, :] = jnp.where(spread[0] == level, spread[1], jnp.zeros_like(level))
        return carry

    lax.fori_loop(0, slots // 16, build_pick, 0)

    def build_onehot():
        for f in range(6):
            code = near[f : f + 1, :]
            own_tile[f], own_hit[f] = tile_of(code)
            at = jnp.where(code >= slots + cap, code - (slots + cap - SIDE), code - slots)
            side_tile[f], side_hit[f] = tile_of(jnp.where(code >= slots, at, -1))

        def body(k, carry):
            rows = pl.ds(pl.multiple_of(k * 16, 16), 16)
            level = jnp.full((16, slots), k.astype(f32)).astype(bf16)
            for f in range(6):
                onehot[f, rows, :] = jnp.where(own_tile[f] == level, own_hit[f], jnp.zeros_like(level))
            return carry

        lax.fori_loop(0, slots // 16, body, 0)

        def side_body(k, carry):
            rows = pl.ds(pl.multiple_of(k * 16, 16), 16)
            level = jnp.full((16, slots), k.astype(f32)).astype(bf16)
            total = jnp.zeros_like(level)
            for f in range(6):
                total = total + jnp.where(side_tile[f] == level, side_hit[f] * (f + 1.0), jnp.zeros_like(level))
            onehot[6, pl.ds(pl.multiple_of(k * 16, 16), 16), :] = total
            return carry

        lax.fori_loop(0, 2 * SIDE // 16, side_body, 0)
        ones = jnp.ones((16, slots), bf16)
        face_at[...] = lax.dot_general(
            ones, onehot[6], (((1,), (1,)), ((), ())), preferred_element_type=f32
        )

        def side_ones(k, carry):
            rows = pl.ds(pl.multiple_of(k * 16, 16), 16)
            onehot[6, rows, :] = jnp.minimum(onehot[6, rows, :], jnp.ones((16, slots), bf16))
            return carry

        lax.fori_loop(0, 2 * SIDE // 16, side_ones, 0)

    def inner_of(f):
        return jnp.where(near[f : f + 1, :] >= 0, 1.0, 0.0)

    def copy_out(phase, side, piece):
        other = upper if side else lower
        return pltpu.make_async_remote_copy(
            src_ref=out_buf.at[phase, side, piece],
            dst_ref=in_buf.at[phase, 1 - side, piece],
            send_sem=send_sem.at[phase, side, piece],
            recv_sem=recv_sem.at[phase, 1 - side, piece],
            device_id={"dom": other},
            device_id_type=MESH,
        )

    pieces = [(side, piece) for piece in range(SIDE // 256) for side in range(2)]

    def send(phase):
        rows = traces[...].reshape(576, slots)
        for number, (side, piece) in enumerate(pieces):
            start = side * SIDE + piece * 256
            got = dot(rows, pick[:, start : start + 256])
            face = face_of[:, start : start + 256]
            total = jnp.zeros((48, 256), f32)
            for f in range(6):
                both = got[f * 96 : f * 96 + 48] + got[f * 96 + 48 : f * 96 + 96]
                total = jnp.where(face == f, both, total)
            out_buf[phase, side, piece] = total
            if number % 2:
                for end in range(2):
                    copy_out(phase, end, piece).start()

    def own(phase):
        for f in range(6):
            got = dot(traces[f ^ 1], onehot[f, 0:slots, :])
            mine = traces[f, 0:48].astype(f32) + traces[f, 48:96].astype(f32)
            weight = inner_of(f) if phase == 0 else 2.0 - inner_of(f)
            jump[f] = got[0:48] + got[48:96] - mine * weight

    def arrive(phase):
        for side, piece in pieces:
            copy_out(phase, side, piece).wait()
        for side, piece in pieces:
            start = side * SIDE + piece * 256
            columns = slice(start, start + 256)
            high, low = split(in_buf[phase, side, piece])
            for f in range(6):
                chosen = jnp.broadcast_to(
                    jnp.where(face_at[0:1, columns] == f + 1.0, 1.0, 0.0), (16, 256)
                ).astype(bf16)
                for c in range(3):
                    rows = slice(c * 16, c * 16 + 16)
                    halves[f * 96 + c * 16 : f * 96 + c * 16 + 16, columns] = high[rows] * chosen
                    halves[f * 96 + 48 + c * 16 : f * 96 + 64 + c * 16, columns] = low[rows] * chosen
        for t in range(0, slots, 256):
            columns = slice(t, t + 256)
            got = dot(halves[...], onehot[6, :, columns])
            for f in range(6):
                total = jump[f, :, columns] + got[f * 96 : f * 96 + 48] + got[f * 96 + 48 : f * 96 + 96]
                high, low = split(total)
                for c in range(3):
                    jump_in[c, f * 16 : f * 16 + 16, columns] = high[c * 16 : c * 16 + 16]
                    jump_in[c, 96 + f * 16 : 112 + f * 16, columns] = low[c * 16 : c * 16 + 16]

    def put3(ref, index, high, low):
        ref[index, 0:64] = high
        ref[index, 64:128] = high
        ref[index, 128:192] = low

    def put_traces(field, pairs):
        for h in range(0, slots, HALF):
            columns = slice(h, h + HALF)
            tiles = [field[k * 8 : k * 8 + 8, columns] for k in range(8)]
            for c, d in pairs:
                for end, rows in enumerate(face_rows(tiles, d)):
                    high, low = split(jnp.concatenate(rows, axis=0))
                    traces[2 * d + end, c * 16 : c * 16 + 16, columns] = high
                    traces[2 * d + end, 48 + c * 16 : 64 + c * 16, columns] = low

    def velocity_traces():
        for c in range(3):
            put_traces(vel.at[c], [(c, d) for d in range(3)])

    def stress_traces():
        for m, pairs in enumerate(
            (((0, 0),), ((1, 1),), ((2, 2),), ((1, 0), (0, 1)), ((2, 0), (0, 2)), ((2, 1), (1, 2)))
        ):
            put_traces(sig.at[m], pairs)

    blocks = [
        (r, slice(r, r + 8), slice(h, h + HALF)) for r in range(0, 64, 8) for h in range(0, slots, HALF)
    ]

    def step(n, carry):
        velocity_traces()

        @pl.when(n == 0)
        def _():
            pl.semaphore_wait(barrier, 2 + len(peers))

        send(0)

        @pl.when(n == 0)
        def _():
            build_onehot()
            load_s.wait()
            for c in range(6):
                sig[c] = sig[c] * valid
            load_f.wait()

        own(0)
        for c in range(3):
            high, low = split(vel[c])
            put3(field_in, c, high, low)
        for c in range(3):
            high, low = split(forward[n, c])
            fgrad[c] = dot(stage_v[...], jnp.concatenate([high, high, low], axis=0))
            grad[c] = dot(stage_v[...], field_in[c])
        arrive(0)
        for c in range(3):
            got = dot(stage_j[...], jump_in[c])
            impulse[c] = got[0:192]
            kick[c] = got[192:256]
        for r, rows, cols in blocks:
            g = [
                [
                    grad[i, j * 64 + r : j * 64 + r + 8, cols] + impulse[i, j * 64 + r : j * 64 + r + 8, cols]
                    for j in range(3)
                ]
                for i in range(3)
            ]
            shear = mu[rows, cols] * time_step
            bulk = lam[rows, cols] * time_step * (g[0][0] + g[1][1] + g[2][2])
            for c in range(3):
                sig[c, rows, cols] = sig[c, rows, cols] + (bulk + 2.0 * shear * g[c][c])
            for m, (i, j) in ((3, (0, 1)), (4, (0, 2)), (5, (1, 2))):
                sig[m, rows, cols] = sig[m, rows, cols] + shear * (g[i][j] + g[j][i])
        stress_traces()
        send(1)
        for r, rows, cols in blocks:
            g = [[fgrad[i, j * 64 + r : j * 64 + r + 8, cols] for j in range(3)] for i in range(3)]
            s = [sig[m, rows, cols] for m in range(6)]
            rate = g[0][0] + g[1][1] + g[2][2]
            acc[1, rows, cols] = acc[1, rows, cols] - time_step * rate * (s[0] + s[1] + s[2])
            contraction = g[0][0] * s[0] + g[1][1] * s[1] + g[2][2] * s[2]
            contraction = contraction + (g[0][1] + g[1][0]) * s[3]
            contraction = contraction + (g[0][2] + g[2][0]) * s[4]
            contraction = contraction + (g[1][2] + g[2][1]) * s[5]
            acc[2, rows, cols] = acc[2, rows, cols] - (2.0 * time_step) * contraction

        if SUM_EVENTS:
            @pl.when(n == steps - 1)
            def _():
                for copy in x_copies(0):
                    copy.start()

        own(1)
        for m in range(6):
            high, low = split(sig[m])
            put3(sig_in, m, high, low)
        for c in range(3):
            total = dot(stage_v[0:64], sig_in[symmetric_index[c][0]])
            total = total + dot(stage_v[64:128], sig_in[symmetric_index[c][1]])
            total = total + dot(stage_v[128:192], sig_in[symmetric_index[c][2]])
            div[c] = total
        arrive(1)
        for c in range(3):
            impulse[c, 0:64] = dot(lift2[...], jump_in[c])
        for r, rows, cols in blocks:
            z = jnp.sqrt(rho[rows, cols] * (lam[rows, cols] + 2.0 * mu[rows, cols]))
            scale = time_step / rho[rows, cols]
            total = jnp.zeros_like(z)
            for c in range(3):
                rate = div[c, rows, cols] + impulse[c, rows, cols] + z * kick[c, rows, cols]
                new = vel[c, rows, cols] + scale * rate
                vel[c, rows, cols] = new
                total = total + forward[n, c, rows, cols] * new
            acc[0, rows, cols] = acc[0, rows, cols] - time_step * total
        return carry

    valid = jnp.where(jnp.max(near[...], axis=0, keepdims=True) >= 0, 1.0, 0.0)
    load_v.wait()
    for c in range(3):
        vel[c] = vel[c] * valid
    lax.fori_loop(0, steps, step, 0)
    store_v = pltpu.make_async_copy(vel, vel_hbm.at[0], load_sem.at[0])
    if SUM_EVENTS:
        for copy in x_copies(1):
            copy.start()
    store_v.start()
    if SUM_EVENTS:
        scatter_on(0)
        scatter_on(1)
        gather_in(0)
        gather_in(1)
    else:
        part[...] = acc[...]
    store_v.wait()


def hand_out(vel_in, part_in, vel_out, part_out, vel, part, sem):
    loads = [pltpu.make_async_copy(vel_in, vel, sem.at[0]), pltpu.make_async_copy(part_in, part, sem.at[1])]
    stores = [pltpu.make_async_copy(vel, vel_out, sem.at[2]), pltpu.make_async_copy(part, part_out, sem.at[3])]
    for copy in loads:
        copy.start()
    for load, store in zip(loads, stores):
        load.wait()
        store.start()
    for copy in stores:
        copy.wait()


def local(
    adjoint_state, forward_velocity, density, lame_lambda, shear_modulus, neighbour, send_list
):
    slots = density.shape[1]
    stage_v, stage_j, lift2 = (jnp.asarray(x) for x in tables())
    vmem = pl.BlockSpec(memory_space=pltpu.VMEM)
    hbm = pl.BlockSpec(memory_space=pl.ANY)
    share = 64 * slots // (NX * NZ)
    steps = forward_velocity.shape[1]
    velocity, part = pl.pallas_call(
        sim_kernel,
        out_shape=(
            jax.ShapeDtypeStruct((1, 3, 64, slots), f32),
            jax.ShapeDtypeStruct((3, 1, share) if SUM_EVENTS else (3, 64, slots), f32),
        ),
        in_specs=[hbm] * 2 + [vmem] * 8,
        out_specs=(hbm, vmem),
        scratch_shapes=[
            pltpu.VMEM((3, 64, slots), f32),
            pltpu.VMEM((steps, 3, 64, slots), f32),
            pltpu.VMEM((3, 64, slots), f32),
            pltpu.VMEM((6, 64, slots), f32),
            pltpu.VMEM((7, 2 * SIDE, slots), bf16),
            pltpu.VMEM((slots, 2 * SIDE), bf16),
            pltpu.VMEM((2, 16, 2 * SIDE), bf16),
            pltpu.VMEM((6, 16, slots), bf16),
            pltpu.VMEM((6, 16, slots), bf16),
            pltpu.VMEM((6, 16, slots), bf16),
            pltpu.VMEM((6, 16, slots), bf16),
            pltpu.VMEM((8, 2 * SIDE), jnp.int32),
            pltpu.VMEM((6, 96, slots), bf16),
            pltpu.VMEM((6, 48, slots), f32),
            pltpu.VMEM((3, 192, slots), bf16),
            pltpu.VMEM((3, 192, slots), bf16),
            pltpu.VMEM((3, 192, slots), f32),
            pltpu.VMEM((3, 64, slots), f32),
            pltpu.VMEM((3, 192, slots), f32),
            pltpu.VMEM((6, 192, slots), bf16),
            pltpu.VMEM((3, 192, slots), f32),
            pltpu.VMEM((3, 64, slots), f32),
            pltpu.VMEM((576, 2 * SIDE), bf16),
            pltpu.VMEM((16, 2 * SIDE), f32),
            pltpu.VMEM((2, 2, SIDE // 256, 48, 256), f32),
            pltpu.VMEM((2, 2, SIDE // 256, 48, 256), f32),
            pltpu.VMEM((NX - 1, 3, 64 // NX, slots), f32),
            pltpu.VMEM((3, 64 // NX, slots), f32),
            pltpu.VMEM((NZ, 3, share // 128, 128), f32),
            pltpu.VMEM((NZ - 1, 3, share // 128, 128), f32),
            pltpu.SemaphoreType.DMA((3,)),
            pltpu.SemaphoreType.DMA((2, 2, SIDE // 256)),
            pltpu.SemaphoreType.DMA((2, 2, SIDE // 256)),
            pltpu.SemaphoreType.DMA((2, NX - 1)),
            pltpu.SemaphoreType.DMA((2, NX - 1)),
            pltpu.SemaphoreType.DMA((2, NZ - 1)),
            pltpu.SemaphoreType.DMA((2, NZ - 1)),
        ],
        compiler_params=pltpu.CompilerParams(
            collective_id=0, has_side_effects=True, vmem_limit_bytes=60 * 1024 * 1024
        ),
    )(
        adjoint_state, forward_velocity, density, lame_lambda, shear_modulus, neighbour, send_list,
        stage_v, stage_j, lift2,
    )
    if not SUM_EVENTS:
        part = part.reshape(3, 1, -1)
    return pl.pallas_call(
        hand_out,
        out_shape=tuple(jax.ShapeDtypeStruct(x.shape, f32) for x in (velocity, part)),
        in_specs=[hbm, hbm],
        out_specs=(hbm, hbm),
        scratch_shapes=[
            pltpu.VMEM(velocity.shape, f32),
            pltpu.VMEM(part.shape, f32),
            pltpu.SemaphoreType.DMA((4,)),
        ],
    )(velocity, part)


def solution(mesh):
    placed = (
        P("event", None, None, "dom"),
        P("event", None, None, None, "dom"),
        P(None, "dom"),
        P(None, "dom"),
        P(None, "dom"),
        P(None, "dom"),
        P(None, "dom"),
    )
    return jax.shard_map(
        local,
        mesh=mesh,
        in_specs=placed,
        out_specs=(P("event", None, None, "dom"), P(None, "dom", "event")),
        check_vma=False,
    )
```

```python
import functools
import math

import jax
import jax.numpy as jnp
import numpy as np
from jax import lax
from jax.experimental import pallas as pl
from jax.experimental.pallas import tpu as pltpu
from jax.sharding import PartitionSpec as P
import ml_dtypes

time_step = 0.02
half_lift = 3.0
symmetric_index = ((0, 3, 4), (3, 1, 5), (4, 5, 2))
SIDE = 512
HALF = 384
NX, NZ = 4, 12
SUM_EVENTS = True
MESH = pl.DeviceIdType.MESH
f32 = jnp.float32
bf16 = jnp.bfloat16


def lobatto_diff():
    points = [-1.0, -1.0 / math.sqrt(5.0), 1.0 / math.sqrt(5.0), 1.0]
    weights = [
        1.0 / math.prod([points[target] - points[other] for other in range(4) if other != target])
        for target in range(4)
    ]
    offdiag = [
        [
            (
                0.0
                if target == source
                else weights[source] / weights[target] / (points[target] - points[source])
            )
            for source in range(4)
        ]
        for target in range(4)
    ]
    return np.array(
        [
            [
                -sum(offdiag[target]) if target == source else offdiag[target][source]
                for source in range(4)
            ]
            for target in range(4)
        ],
        dtype=np.float32,
    )


def deriv_table():
    matrix = lobatto_diff()
    identity = np.eye(4, dtype=np.float32)
    return np.concatenate(
        [
            np.kron(np.kron(matrix, identity), identity),
            np.kron(np.kron(identity, matrix), identity),
            np.kron(np.kron(identity, identity), matrix),
        ],
        axis=0,
    ).astype(np.float32)


def face_nodes():
    nodes = np.zeros((6, 16), np.int32)
    for face in range(6):
        for q in range(16):
            coordinates = [q // 4, q % 4]
            coordinates.insert(face // 2, 3 * (face % 2))
            nodes[face, q] = 16 * coordinates[0] + 4 * coordinates[1] + coordinates[2]
    return nodes


def tables():
    to_bf16 = lambda x: np.asarray(x, np.float32).astype(ml_dtypes.bfloat16)
    deriv = deriv_table()
    high = to_bf16(deriv)
    low = to_bf16(deriv - high.astype(np.float32))
    deriv3 = np.concatenate([high, low, high], axis=1)
    nodes = face_nodes()
    signed = np.zeros((192, 96), np.float32)
    summed = np.zeros((64, 96), np.float32)
    plain = np.zeros((64, 96), np.float32)
    for face in range(6):
        sign = face % 2 * 2 - 1.0
        for q in range(16):
            column, node = face * 16 + q, nodes[face, q]
            signed[face // 2 * 64 + node, column] = half_lift * sign
            summed[node, column] = half_lift * sign
            plain[node, column] = half_lift
    stage_j = np.concatenate([signed, plain], axis=0)
    stage_j = np.concatenate([stage_j, stage_j], axis=1)
    lift2 = np.concatenate([summed, summed], axis=1)
    return deriv3, to_bf16(stage_j), to_bf16(lift2)


def split(x):
    high = x.astype(bf16)
    return high, (x - high.astype(f32)).astype(bf16)


def face_rows(tiles, dim):
    if dim == 0:
        return tiles[0:2], tiles[6:8]
    sub = lax.broadcasted_iota(jnp.int32, tiles[0].shape, 0)
    roll = lambda x, by: pltpu.roll(x, by % 8, 0) if by % 8 else x
    if dim == 1:
        low = [jnp.where(sub < 4, tiles[k], roll(tiles[k + 2], 4)) for k in (0, 4)]
        high = [jnp.where(sub < 4, roll(tiles[k + 1], 4), tiles[k + 3]) for k in (0, 4)]
        return low, high
    out = []
    for start in (0, 3):
        rows = []
        for k in (0, 4):
            total = roll(tiles[k], -start)
            for q in range(1, 8):
                total = jnp.where(sub == q, roll(tiles[k + q // 2], q - start - q % 2 * 4), total)
            rows.append(total)
        out.append(rows)
    return out


def dot(a, b):
    return jnp.dot(a, b, preferred_element_type=f32)


def sim_kernel(
    state, forward_hbm, rho, lam, mu, near, sends, stage_v, stage_j, lift2,
    vel_hbm, part,
    vel, forward, acc, sig, onehot, pick, spread, own_tile, own_hit, side_tile, side_hit, send_ids,
    traces, jump, field_in, jump_in, grad, kick, fgrad, sig_in, impulse, div, halves, chosen_at,
    out_buf, in_buf, x_in, x_sum, z_out, z_in,
    load_sem, send_sem, recv_sem, x_send, x_recv, z_send, z_recv,
):
    count = lax.axis_size("dom")
    me = lax.axis_index("dom")
    lower = lax.rem(me + count - 1, count)
    upper = lax.rem(me + 1, count)
    slots = rho.shape[1]
    cap = sends.shape[1]
    steps = forward.shape[0]

    load_v = pltpu.make_async_copy(state.at[0, 0:3], vel, load_sem.at[0])
    load_s = pltpu.make_async_copy(state.at[0, 3:9], sig, load_sem.at[1])
    load_f = pltpu.make_async_copy(forward_hbm.at[0], forward, load_sem.at[2])
    load_v.start()
    load_s.start()
    load_f.start()

    barrier = pltpu.get_barrier_semaphore()
    for other in (lower, upper):
        pl.semaphore_signal(barrier, inc=1, device_id={"dom": other}, device_id_type=MESH)
    event = lax.axis_index("event")
    along_x, along_z = event // NZ, lax.rem(event, NZ)
    x_peers = [lax.rem(along_x + d, NX) for d in range(1, NX)]
    z_peers = [lax.rem(along_z + d, NZ) for d in range(1, NZ)]
    peers = [p * NZ + along_z for p in x_peers] + [along_x * NZ + p for p in z_peers]
    if not SUM_EVENTS:
        peers = []
    for other in peers:
        pl.semaphore_signal(barrier, inc=1, device_id={"event": other}, device_id_type=MESH)
    band = 64 // NX

    def x_copies(group):
        terms = slice(1, 3) if group == 0 else slice(0, 1)
        return [
            pltpu.make_async_remote_copy(
                src_ref=acc.at[terms, pl.ds(pl.multiple_of(p * band, band), band), :],
                dst_ref=x_in.at[d, terms],
                send_sem=x_send.at[group, d],
                recv_sem=x_recv.at[group, d],
                device_id={"event": p * NZ + along_z},
                device_id_type=MESH,
            )
            for d, p in enumerate(x_peers)
        ]

    def z_copies(group):
        terms = slice(1, 3) if group == 0 else slice(0, 1)
        return [
            pltpu.make_async_remote_copy(
                src_ref=z_out.at[p, terms],
                dst_ref=z_in.at[d, terms],
                send_sem=z_send.at[group, d],
                recv_sem=z_recv.at[group, d],
                device_id={"event": along_x * NZ + p},
                device_id_type=MESH,
            )
            for d, p in enumerate(z_peers)
        ]

    def scatter_on(group):
        for copy in x_copies(group):
            copy.wait()
        mine = pl.ds(pl.multiple_of(along_x * band, band), band)
        for t in (1, 2) if group == 0 else (0,):
            total = acc[t, mine, :]
            for d in range(NX - 1):
                total = total + x_in[d, t]
            x_sum[t] = total
            for piece in range(band * slots // 128):
                row, column = piece // (slots // 128), piece % (slots // 128) * 128
                z_out[piece // 8, t, piece % 8 : piece % 8 + 1, :] = x_sum[t, row : row + 1, column : column + 128]
        for copy in z_copies(group):
            copy.start()

    def gather_in(group):
        for copy in z_copies(group):
            copy.wait()
        for t in (1, 2) if group == 0 else (0,):
            total = z_out[along_z, t]
            for d in range(NZ - 1):
                total = total + z_in[d, t]
            for row in range(8):
                part[t, :, row * 128 : row * 128 + 128] = total[row : row + 1, :]

    acc[...] = jnp.zeros_like(acc)

    send_ids[...] = jnp.full_like(send_ids, -1)
    send_ids[0:1, 0:cap] = sends[0:1, :]
    send_ids[0:1, SIDE : SIDE + cap] = sends[1:2, :]
    ids = send_ids[0:1, :]
    face_of = jnp.where(ids < 0, -1, 0)
    for f in range(1, 6):
        face_of = face_of + jnp.where(ids >= f * slots, 1, 0)
    slot_of = jnp.where(ids < 0, -1, ids - face_of * slots)

    def tile_of(index):
        width = index.shape[1]
        tile = jnp.right_shift(index, 4)
        row = lax.broadcasted_iota(jnp.int32, (16, width), 0)
        hit = jnp.where(jnp.bitwise_and(index, 15) == row, 1.0, 0.0)
        return jnp.broadcast_to(tile.astype(f32), (16, width)).astype(bf16), hit.astype(bf16)

    spread[0], spread[1] = tile_of(slot_of)

    def build_pick(k, carry):
        rows = pl.ds(pl.multiple_of(k * 16, 16), 16)
        level = jnp.full((16, 2 * SIDE), k.astype(f32)).astype(bf16)
        pick[rows, :] = jnp.where(spread[0] == level, spread[1], jnp.zeros_like(level))
        return carry

    lax.fori_loop(0, slots // 16, build_pick, 0)

    def build_onehot():
        for f in range(6):
            code = near[f : f + 1, :]
            own_tile[f], own_hit[f] = tile_of(code)
            side = jnp.where(code >= slots + cap, 1, 0)
            at = code - slots - side * cap
            at = at + jnp.right_shift(at, 8) * 256 + side * 256
            side_tile[f], side_hit[f] = tile_of(jnp.where(code >= slots, at, -1))

        def body(k, carry):
            rows = pl.ds(pl.multiple_of(k * 16, 16), 16)
            level = jnp.full((16, slots), k.astype(f32)).astype(bf16)
            for f in range(6):
                onehot[f, rows, :] = jnp.where(own_tile[f] == level, own_hit[f], jnp.zeros_like(level))
            return carry

        lax.fori_loop(0, slots // 16, body, 0)

        def side_body(k, carry):
            rows = pl.ds(pl.multiple_of(k * 16, 16), 16)
            level = jnp.full((16, slots), k.astype(f32)).astype(bf16)
            total = jnp.zeros_like(level)
            for f in range(6):
                total = total + jnp.where(side_tile[f] == level, side_hit[f] * (f + 1.0), jnp.zeros_like(level))
            onehot[6, pl.ds(pl.multiple_of(k * 16, 16), 16), :] = total
            return carry

        lax.fori_loop(0, 2 * SIDE // 16, side_body, 0)
        ones = jnp.ones((16, slots), bf16)
        face_at = lax.dot_general(
            ones, onehot[6], (((1,), (1,)), ((), ())), preferred_element_type=f32
        )
        for f in range(6):
            chosen_at[f] = jnp.where(face_at == f + 1.0, 1.0, 0.0).astype(bf16)

        def side_ones(k, carry):
            rows = pl.ds(pl.multiple_of(k * 16, 16), 16)
            onehot[6, rows, :] = jnp.minimum(onehot[6, rows, :], jnp.ones((16, slots), bf16))
            return carry

        lax.fori_loop(0, 2 * SIDE // 16, side_ones, 0)

    def inner_of(f):
        return jnp.where(near[f : f + 1, :] >= 0, 1.0, 0.0)

    def copy_out(phase, side, piece):
        other = upper if side else lower
        return pltpu.make_async_remote_copy(
            src_ref=out_buf.at[phase, side, piece],
            dst_ref=in_buf.at[phase, 1 - side, piece],
            send_sem=send_sem.at[phase, side, piece],
            recv_sem=recv_sem.at[phase, 1 - side, piece],
            device_id={"dom": other},
            device_id_type=MESH,
        )

    pieces = [(side, piece) for piece in range(SIDE // 256) for side in range(2)]

    def send(phase, n):
        rows = traces[...].reshape(576, slots)
        for number, (side, piece) in enumerate(pieces):
            start = side * SIDE + piece * 256
            got = dot(rows, pick[:, start : start + 256])
            face = face_of[:, start : start + 256]
            total = jnp.zeros((48, 256), f32)
            for f in range(6):
                both = got[f * 96 : f * 96 + 48] + got[f * 96 + 48 : f * 96 + 96]
                total = jnp.where(face == f, both, total)
            out_buf[phase, side, piece] = total
            if phase == 0 and number == 1:
                @pl.when(n == 0)
                def _():
                    pl.semaphore_wait(barrier, 2 + len(peers))

            if number % 2:
                for end in range(2):
                    copy_out(phase, end, piece).start()

    def own(phase):
        for f in range(6):
            got = dot(traces[f ^ 1], onehot[f, 0:slots, :])
            mine = traces[f, 0:48].astype(f32) + traces[f, 48:96].astype(f32)
            weight = inner_of(f) if phase == 0 else 2.0 - inner_of(f)
            jump[f] = got[0:48] + got[48:96] - mine * weight

    def arrive(phase):
        last = SIDE // 256 - 1
        for piece in range(last + 1):
            for side in range(2):
                copy_out(phase, side, piece).wait()
            for side in range(2):
                start = piece * 512 + side * 256
                columns = slice(start, start + 256)
                high, low = split(in_buf[phase, side, piece])
                for f in range(6):
                    chosen = chosen_at[f, :, columns]
                    for c in range(3):
                        rows = slice(c * 16, c * 16 + 16)
                        halves[f * 96 + c * 16 : f * 96 + c * 16 + 16, columns] = high[rows] * chosen
                        halves[f * 96 + 48 + c * 16 : f * 96 + 64 + c * 16, columns] = low[rows] * chosen
            both = slice(piece * 512, piece * 512 + 512)
            for t in range(0, slots, 256):
                columns = slice(t, t + 256)
                got = dot(halves[:, both], onehot[6, both, columns])
                for f in range(6):
                    total = jump[f, :, columns] + got[f * 96 : f * 96 + 48] + got[f * 96 + 48 : f * 96 + 96]
                    if piece < last:
                        jump[f, :, columns] = total
                        continue
                    high, low = split(total)
                    for c in range(3):
                        jump_in[c, f * 16 : f * 16 + 16, columns] = high[c * 16 : c * 16 + 16]
                        jump_in[c, 96 + f * 16 : 112 + f * 16, columns] = low[c * 16 : c * 16 + 16]

    def put3(ref, index, high, low):
        ref[index, 0:64] = high
        ref[index, 64:128] = high
        ref[index, 128:192] = low

    def put_traces(field, pairs):
        for h in range(0, slots, HALF):
            columns = slice(h, h + HALF)
            tiles = [field[k * 8 : k * 8 + 8, columns] for k in range(8)]
            for c, d in pairs:
                for end, rows in enumerate(face_rows(tiles, d)):
                    high, low = split(jnp.concatenate(rows, axis=0))
                    traces[2 * d + end, c * 16 : c * 16 + 16, columns] = high
                    traces[2 * d + end, 48 + c * 16 : 64 + c * 16, columns] = low

    def velocity_traces():
        for c in range(3):
            put_traces(vel.at[c], [(c, d) for d in range(3)])

    def stress_traces():
        for m, pairs in enumerate(
            (((0, 0),), ((1, 1),), ((2, 2),), ((1, 0), (0, 1)), ((2, 0), (0, 2)), ((2, 1), (1, 2)))
        ):
            put_traces(sig.at[m], pairs)

    blocks = [
        (r, slice(r, r + 8), slice(h, h + HALF)) for r in range(0, 64, 8) for h in range(0, slots, HALF)
    ]

    def step(n, carry):
        velocity_traces()

        send(0, n)

        @pl.when(n == 0)
        def _():
            build_onehot()
            load_s.wait()
            for c in range(6):
                sig[c] = sig[c] * valid
            load_f.wait()

        own(0)
        for c in range(3):
            high, low = split(vel[c])
            put3(field_in, c, high, low)
        for c in range(3):
            high, low = split(forward[n, c])
            fgrad[c] = dot(stage_v[...], jnp.concatenate([high, high, low], axis=0))
            grad[c] = dot(stage_v[...], field_in[c])
        arrive(0)
        for c in range(3):
            got = dot(stage_j[...], jump_in[c])
            impulse[c] = got[0:192]
            kick[c] = got[192:256]
        for r, rows, cols in blocks:
            g = [
                [
                    grad[i, j * 64 + r : j * 64 + r + 8, cols] + impulse[i, j * 64 + r : j * 64 + r + 8, cols]
                    for j in range(3)
                ]
                for i in range(3)
            ]
            shear = mu[rows, cols] * time_step
            bulk = lam[rows, cols] * time_step * (g[0][0] + g[1][1] + g[2][2])
            for c in range(3):
                sig[c, rows, cols] = sig[c, rows, cols] + (bulk + 2.0 * shear * g[c][c])
            for m, (i, j) in ((3, (0, 1)), (4, (0, 2)), (5, (1, 2))):
                sig[m, rows, cols] = sig[m, rows, cols] + shear * (g[i][j] + g[j][i])
        stress_traces()
        send(1, n)
        for r, rows, cols in blocks:
            g = [[fgrad[i, j * 64 + r : j * 64 + r + 8, cols] for j in range(3)] for i in range(3)]
            s = [sig[m, rows, cols] for m in range(6)]
            rate = g[0][0] + g[1][1] + g[2][2]
            acc[1, rows, cols] = acc[1, rows, cols] - time_step * rate * (s[0] + s[1] + s[2])
            contraction = g[0][0] * s[0] + g[1][1] * s[1] + g[2][2] * s[2]
            contraction = contraction + (g[0][1] + g[1][0]) * s[3]
            contraction = contraction + (g[0][2] + g[2][0]) * s[4]
            contraction = contraction + (g[1][2] + g[2][1]) * s[5]
            acc[2, rows, cols] = acc[2, rows, cols] - (2.0 * time_step) * contraction

        if SUM_EVENTS:
            @pl.when(n == steps - 1)
            def _():
                for copy in x_copies(0):
                    copy.start()

        own(1)
        for m in range(6):
            high, low = split(sig[m])
            put3(sig_in, m, high, low)
        for c in range(3):
            total = dot(stage_v[0:64], sig_in[symmetric_index[c][0]])
            total = total + dot(stage_v[64:128], sig_in[symmetric_index[c][1]])
            total = total + dot(stage_v[128:192], sig_in[symmetric_index[c][2]])
            div[c] = total
        arrive(1)
        for c in range(3):
            impulse[c, 0:64] = dot(lift2[...], jump_in[c])
        for r, rows, cols in blocks:
            z = jnp.sqrt(rho[rows, cols] * (lam[rows, cols] + 2.0 * mu[rows, cols]))
            scale = time_step / rho[rows, cols]
            total = jnp.zeros_like(z)
            for c in range(3):
                rate = div[c, rows, cols] + impulse[c, rows, cols] + z * kick[c, rows, cols]
                new = vel[c, rows, cols] + scale * rate
                vel[c, rows, cols] = new
                total = total + forward[n, c, rows, cols] * new
            acc[0, rows, cols] = acc[0, rows, cols] - time_step * total
        return carry

    valid = jnp.where(jnp.max(near[...], axis=0, keepdims=True) >= 0, 1.0, 0.0)
    load_v.wait()
    for c in range(3):
        vel[c] = vel[c] * valid
    lax.fori_loop(0, steps, step, 0)
    store_v = pltpu.make_async_copy(vel, vel_hbm.at[0], load_sem.at[0])
    if SUM_EVENTS:
        for copy in x_copies(1):
            copy.start()
    store_v.start()
    if SUM_EVENTS:
        scatter_on(0)
        scatter_on(1)
        gather_in(0)
        gather_in(1)
    else:
        part[...] = acc[...]
    store_v.wait()


def hand_out(vel_in, part_in, vel_out, part_out, vel, part, sem):
    loads = [pltpu.make_async_copy(vel_in.at[0, c], vel.at[c], sem.at[0, c]) for c in range(3)]
    loads.append(pltpu.make_async_copy(part_in, part, sem.at[0, 3]))
    stores = [pltpu.make_async_copy(vel.at[c], vel_out.at[0, c], sem.at[1, c]) for c in range(3)]
    stores.append(pltpu.make_async_copy(part, part_out, sem.at[1, 3]))
    for copy in loads:
        copy.start()
    for load, store in zip(loads, stores):
        load.wait()
        store.start()
    for copy in stores:
        copy.wait()


def local(
    adjoint_state, forward_velocity, density, lame_lambda, shear_modulus, neighbour, send_list
):
    slots = density.shape[1]
    stage_v, stage_j, lift2 = (jnp.asarray(x) for x in tables())
    vmem = pl.BlockSpec(memory_space=pltpu.VMEM)
    hbm = pl.BlockSpec(memory_space=pl.ANY)
    share = 64 * slots // (NX * NZ)
    steps = forward_velocity.shape[1]
    velocity, part = pl.pallas_call(
        sim_kernel,
        out_shape=(
            jax.ShapeDtypeStruct((1, 3, 64, slots), f32),
            jax.ShapeDtypeStruct((3, 1, share) if SUM_EVENTS else (3, 64, slots), f32),
        ),
        in_specs=[hbm] * 2 + [vmem] * 8,
        out_specs=(hbm, vmem),
        scratch_shapes=[
            pltpu.VMEM((3, 64, slots), f32),
            pltpu.VMEM((steps, 3, 64, slots), f32),
            pltpu.VMEM((3, 64, slots), f32),
            pltpu.VMEM((6, 64, slots), f32),
            pltpu.VMEM((7, 2 * SIDE, slots), bf16),
            pltpu.VMEM((slots, 2 * SIDE), bf16),
            pltpu.VMEM((2, 16, 2 * SIDE), bf16),
            pltpu.VMEM((6, 16, slots), bf16),
            pltpu.VMEM((6, 16, slots), bf16),
            pltpu.VMEM((6, 16, slots), bf16),
            pltpu.VMEM((6, 16, slots), bf16),
            pltpu.VMEM((8, 2 * SIDE), jnp.int32),
            pltpu.VMEM((6, 96, slots), bf16),
            pltpu.VMEM((6, 48, slots), f32),
            pltpu.VMEM((3, 192, slots), bf16),
            pltpu.VMEM((3, 192, slots), bf16),
            pltpu.VMEM((3, 192, slots), f32),
            pltpu.VMEM((3, 64, slots), f32),
            pltpu.VMEM((3, 192, slots), f32),
            pltpu.VMEM((6, 192, slots), bf16),
            pltpu.VMEM((3, 192, slots), f32),
            pltpu.VMEM((3, 64, slots), f32),
            pltpu.VMEM((576, 2 * SIDE), bf16),
            pltpu.VMEM((6, 16, 2 * SIDE), bf16),
            pltpu.VMEM((2, 2, SIDE // 256, 48, 256), f32),
            pltpu.VMEM((2, 2, SIDE // 256, 48, 256), f32),
            pltpu.VMEM((NX - 1, 3, 64 // NX, slots), f32),
            pltpu.VMEM((3, 64 // NX, slots), f32),
            pltpu.VMEM((NZ, 3, share // 128, 128), f32),
            pltpu.VMEM((NZ - 1, 3, share // 128, 128), f32),
            pltpu.SemaphoreType.DMA((3,)),
            pltpu.SemaphoreType.DMA((2, 2, SIDE // 256)),
            pltpu.SemaphoreType.DMA((2, 2, SIDE // 256)),
            pltpu.SemaphoreType.DMA((2, NX - 1)),
            pltpu.SemaphoreType.DMA((2, NX - 1)),
            pltpu.SemaphoreType.DMA((2, NZ - 1)),
            pltpu.SemaphoreType.DMA((2, NZ - 1)),
        ],
        compiler_params=pltpu.CompilerParams(
            collective_id=0, has_side_effects=True, vmem_limit_bytes=60 * 1024 * 1024
        ),
    )(
        adjoint_state, forward_velocity, density, lame_lambda, shear_modulus, neighbour, send_list,
        stage_v, stage_j, lift2,
    )
    if not SUM_EVENTS:
        part = part.reshape(3, 1, -1)
    return pl.pallas_call(
        hand_out,
        out_shape=tuple(jax.ShapeDtypeStruct(x.shape, f32) for x in (velocity, part)),
        in_specs=[hbm, hbm],
        out_specs=(hbm, hbm),
        scratch_shapes=[
            pltpu.VMEM(velocity.shape[1:], f32),
            pltpu.VMEM(part.shape, f32),
            pltpu.SemaphoreType.DMA((2, 4)),
        ],
    )(velocity, part)


def solution(mesh):
    placed = (
        P("event", None, None, "dom"),
        P("event", None, None, None, "dom"),
        P(None, "dom"),
        P(None, "dom"),
        P(None, "dom"),
        P(None, "dom"),
        P(None, "dom"),
    )
    return jax.shard_map(
        local,
        mesh=mesh,
        in_specs=placed,
        out_specs=(P("event", None, None, "dom"), P(None, "dom", "event")),
        check_vma=False,
    )
```

```python
import functools
import math

import jax
import jax.numpy as jnp
import numpy as np
from jax import lax
from jax.experimental import pallas as pl
from jax.experimental.pallas import tpu as pltpu
from jax.sharding import PartitionSpec as P
import ml_dtypes

time_step = 0.02
half_lift = 3.0
symmetric_index = ((0, 3, 4), (3, 1, 5), (4, 5, 2))
SIDE = 512
PIECE = 128
HALF = 384
NX, NZ = 4, 12
SUM_EVENTS = True
MESH = pl.DeviceIdType.MESH
f32 = jnp.float32
bf16 = jnp.bfloat16


def lobatto_diff():
    points = [-1.0, -1.0 / math.sqrt(5.0), 1.0 / math.sqrt(5.0), 1.0]
    weights = [
        1.0 / math.prod([points[target] - points[other] for other in range(4) if other != target])
        for target in range(4)
    ]
    offdiag = [
        [
            (
                0.0
                if target == source
                else weights[source] / weights[target] / (points[target] - points[source])
            )
            for source in range(4)
        ]
        for target in range(4)
    ]
    return np.array(
        [
            [
                -sum(offdiag[target]) if target == source else offdiag[target][source]
                for source in range(4)
            ]
            for target in range(4)
        ],
        dtype=np.float32,
    )


def deriv_table():
    matrix = lobatto_diff()
    identity = np.eye(4, dtype=np.float32)
    return np.concatenate(
        [
            np.kron(np.kron(matrix, identity), identity),
            np.kron(np.kron(identity, matrix), identity),
            np.kron(np.kron(identity, identity), matrix),
        ],
        axis=0,
    ).astype(np.float32)


def face_nodes():
    nodes = np.zeros((6, 16), np.int32)
    for face in range(6):
        for q in range(16):
            coordinates = [q // 4, q % 4]
            coordinates.insert(face // 2, 3 * (face % 2))
            nodes[face, q] = 16 * coordinates[0] + 4 * coordinates[1] + coordinates[2]
    return nodes


def tables():
    to_bf16 = lambda x: np.asarray(x, np.float32).astype(ml_dtypes.bfloat16)
    deriv = deriv_table()
    high = to_bf16(deriv)
    low = to_bf16(deriv - high.astype(np.float32))
    deriv3 = np.concatenate([high, low, high], axis=1)
    nodes = face_nodes()
    signed = np.zeros((192, 96), np.float32)
    summed = np.zeros((64, 96), np.float32)
    plain = np.zeros((64, 96), np.float32)
    for face in range(6):
        sign = face % 2 * 2 - 1.0
        for q in range(16):
            column, node = face * 16 + q, nodes[face, q]
            signed[face // 2 * 64 + node, column] = half_lift * sign
            summed[node, column] = half_lift * sign
            plain[node, column] = half_lift
    stage_j = np.concatenate([signed, plain], axis=0)
    stage_j = np.concatenate([stage_j, stage_j], axis=1)
    lift2 = np.concatenate([summed, summed], axis=1)
    return deriv3, to_bf16(stage_j), to_bf16(lift2)


def split(x):
    high = x.astype(bf16)
    return high, (x - high.astype(f32)).astype(bf16)


def face_rows(tiles, dim):
    if dim == 0:
        return tiles[0:2], tiles[6:8]
    sub = lax.broadcasted_iota(jnp.int32, tiles[0].shape, 0)
    roll = lambda x, by: pltpu.roll(x, by % 8, 0) if by % 8 else x
    if dim == 1:
        low = [jnp.where(sub < 4, tiles[k], roll(tiles[k + 2], 4)) for k in (0, 4)]
        high = [jnp.where(sub < 4, roll(tiles[k + 1], 4), tiles[k + 3]) for k in (0, 4)]
        return low, high
    out = []
    for start in (0, 3):
        rows = []
        for k in (0, 4):
            total = roll(tiles[k], -start)
            for q in range(1, 8):
                total = jnp.where(sub == q, roll(tiles[k + q // 2], q - start - q % 2 * 4), total)
            rows.append(total)
        out.append(rows)
    return out


def dot(a, b):
    return jnp.dot(a, b, preferred_element_type=f32)


def sim_kernel(
    state, forward_hbm, rho, lam, mu, near, sends, stage_v, stage_j, lift2,
    vel_hbm, part,
    vel, forward, acc, sig, onehot, pick, spread, own_tile, own_hit, side_tile, side_hit, send_ids,
    traces, jump, field_in, jump_in, grad, kick, fgrad, sig_in, impulse, div, halves, chosen_at,
    out_buf, in_buf, x_in, x_sum, z_out, z_in,
    load_sem, send_sem, recv_sem, x_send, x_recv, z_send, z_recv,
):
    count = lax.axis_size("dom")
    me = lax.axis_index("dom")
    lower = lax.rem(me + count - 1, count)
    upper = lax.rem(me + 1, count)
    slots = rho.shape[1]
    cap = sends.shape[1]
    steps = forward.shape[0]

    load_v = pltpu.make_async_copy(state.at[0, 0:3], vel, load_sem.at[0])
    load_s = pltpu.make_async_copy(state.at[0, 3:9], sig, load_sem.at[1])
    load_f = pltpu.make_async_copy(forward_hbm.at[0], forward, load_sem.at[2])
    load_v.start()
    load_s.start()
    load_f.start()

    barrier = pltpu.get_barrier_semaphore()
    for other in (lower, upper):
        pl.semaphore_signal(barrier, inc=1, device_id={"dom": other}, device_id_type=MESH)
    event = lax.axis_index("event")
    along_x, along_z = event // NZ, lax.rem(event, NZ)
    x_peers = [lax.rem(along_x + d, NX) for d in range(1, NX)]
    z_peers = [lax.rem(along_z + d, NZ) for d in range(1, NZ)]
    peers = [p * NZ + along_z for p in x_peers] + [along_x * NZ + p for p in z_peers]
    if not SUM_EVENTS:
        peers = []
    for other in peers:
        pl.semaphore_signal(barrier, inc=1, device_id={"event": other}, device_id_type=MESH)
    band = 64 // NX

    def x_copies(group):
        terms = slice(1, 3) if group == 0 else slice(0, 1)
        return [
            pltpu.make_async_remote_copy(
                src_ref=acc.at[terms, pl.ds(pl.multiple_of(p * band, band), band), :],
                dst_ref=x_in.at[d, terms],
                send_sem=x_send.at[group, d],
                recv_sem=x_recv.at[group, d],
                device_id={"event": p * NZ + along_z},
                device_id_type=MESH,
            )
            for d, p in enumerate(x_peers)
        ]

    def z_copies(group):
        terms = slice(1, 3) if group == 0 else slice(0, 1)
        return [
            pltpu.make_async_remote_copy(
                src_ref=z_out.at[p, terms],
                dst_ref=z_in.at[d, terms],
                send_sem=z_send.at[group, d],
                recv_sem=z_recv.at[group, d],
                device_id={"event": along_x * NZ + p},
                device_id_type=MESH,
            )
            for d, p in enumerate(z_peers)
        ]

    def scatter_on(group):
        for copy in x_copies(group):
            copy.wait()
        mine = pl.ds(pl.multiple_of(along_x * band, band), band)
        for t in (1, 2) if group == 0 else (0,):
            total = acc[t, mine, :]
            for d in range(NX - 1):
                total = total + x_in[d, t]
            x_sum[t] = total
            for piece in range(band * slots // 128):
                row, column = piece // (slots // 128), piece % (slots // 128) * 128
                z_out[piece // 8, t, piece % 8 : piece % 8 + 1, :] = x_sum[t, row : row + 1, column : column + 128]
        for copy in z_copies(group):
            copy.start()

    def gather_in(group):
        for copy in z_copies(group):
            copy.wait()
        for t in (1, 2) if group == 0 else (0,):
            total = z_out[along_z, t]
            for d in range(NZ - 1):
                total = total + z_in[d, t]
            for row in range(8):
                part[t, :, row * 128 : row * 128 + 128] = total[row : row + 1, :]

    acc[...] = jnp.zeros_like(acc)

    send_ids[...] = jnp.full_like(send_ids, -1)
    send_ids[0:1, 0:cap] = sends[0:1, :]
    send_ids[0:1, SIDE : SIDE + cap] = sends[1:2, :]
    ids = send_ids[0:1, :]
    face_of = jnp.where(ids < 0, -1, 0)
    for f in range(1, 6):
        face_of = face_of + jnp.where(ids >= f * slots, 1, 0)
    slot_of = jnp.where(ids < 0, -1, ids - face_of * slots)

    def tile_of(index):
        width = index.shape[1]
        tile = jnp.right_shift(index, 4)
        row = lax.broadcasted_iota(jnp.int32, (16, width), 0)
        hit = jnp.where(jnp.bitwise_and(index, 15) == row, 1.0, 0.0)
        return jnp.broadcast_to(tile.astype(f32), (16, width)).astype(bf16), hit.astype(bf16)

    spread[0], spread[1] = tile_of(slot_of)

    def build_pick(k, carry):
        rows = pl.ds(pl.multiple_of(k * 16, 16), 16)
        level = jnp.full((16, 2 * SIDE), k.astype(f32)).astype(bf16)
        pick[rows, :] = jnp.where(spread[0] == level, spread[1], jnp.zeros_like(level))
        return carry

    lax.fori_loop(0, slots // 16, build_pick, 0, unroll=4)

    def build_onehot():
        for f in range(6):
            code = near[f : f + 1, :]
            own_tile[f], own_hit[f] = tile_of(code)
            side = jnp.where(code >= slots + cap, 1, 0)
            at = code - slots - side * cap
            at = at + jnp.right_shift(at, 7) * PIECE + side * PIECE
            side_tile[f], side_hit[f] = tile_of(jnp.where(code >= slots, at, -1))

        def body(k, carry):
            rows = pl.ds(pl.multiple_of(k * 16, 16), 16)
            level = jnp.full((16, slots), k.astype(f32)).astype(bf16)
            for f in range(6):
                onehot[f, rows, :] = jnp.where(own_tile[f] == level, own_hit[f], jnp.zeros_like(level))
            return carry

        lax.fori_loop(0, slots // 16, body, 0, unroll=2)

        def side_body(k, carry):
            rows = pl.ds(pl.multiple_of(k * 16, 16), 16)
            level = jnp.full((16, slots), k.astype(f32)).astype(bf16)
            total = jnp.zeros_like(level)
            for f in range(6):
                total = total + jnp.where(side_tile[f] == level, side_hit[f] * (f + 1.0), jnp.zeros_like(level))
            onehot[6, pl.ds(pl.multiple_of(k * 16, 16), 16), :] = total
            return carry

        lax.fori_loop(0, 2 * SIDE // 16, side_body, 0, unroll=2)
        ones = jnp.ones((16, slots), bf16)
        face_at = lax.dot_general(
            ones, onehot[6], (((1,), (1,)), ((), ())), preferred_element_type=f32
        )
        for f in range(6):
            chosen_at[f] = jnp.where(face_at == f + 1.0, 1.0, 0.0).astype(bf16)

        def side_ones(k, carry):
            rows = pl.ds(pl.multiple_of(k * 16, 16), 16)
            onehot[6, rows, :] = jnp.minimum(onehot[6, rows, :], jnp.ones((16, slots), bf16))
            return carry

        lax.fori_loop(0, 2 * SIDE // 16, side_ones, 0, unroll=4)

    def inner_of(f):
        return jnp.where(near[f : f + 1, :] >= 0, 1.0, 0.0)

    def copy_out(phase, side, piece):
        other = upper if side else lower
        return pltpu.make_async_remote_copy(
            src_ref=out_buf.at[phase, side, piece],
            dst_ref=in_buf.at[phase, 1 - side, piece],
            send_sem=send_sem.at[phase, side, piece],
            recv_sem=recv_sem.at[phase, 1 - side, piece],
            device_id={"dom": other},
            device_id_type=MESH,
        )

    pieces = [(side, piece) for piece in range(SIDE // 256) for side in range(2)]

    def send(phase, n):
        rows = traces[...].reshape(576, slots)
        for number, (side, piece) in enumerate(pieces):
            start = side * SIDE + piece * 256
            got = dot(rows, pick[:, start : start + 256])
            face = face_of[:, start : start + 256]
            total = jnp.zeros((48, 256), f32)
            for f in range(6):
                both = got[f * 96 : f * 96 + 48] + got[f * 96 + 48 : f * 96 + 96]
                total = jnp.where(face == f, both, total)
            for k in range(256 // PIECE):
                out_buf[phase, side, piece * (256 // PIECE) + k] = total[:, k * PIECE : k * PIECE + PIECE]
            if phase == 0 and number == 1:
                @pl.when(n == 0)
                def _():
                    pl.semaphore_wait(barrier, 2 + len(peers))

            if number % 2:
                for k in range(256 // PIECE):
                    for end in range(2):
                        copy_out(phase, end, piece * (256 // PIECE) + k).start()

    def own(phase):
        for f in range(6):
            got = dot(traces[f ^ 1], onehot[f, 0:slots, :])
            mine = traces[f, 0:48].astype(f32) + traces[f, 48:96].astype(f32)
            weight = inner_of(f) if phase == 0 else 2.0 - inner_of(f)
            jump[f] = got[0:48] + got[48:96] - mine * weight

    def arrive(phase):
        last = SIDE // PIECE - 1
        for piece in range(last + 1):
            for side in range(2):
                copy_out(phase, side, piece).wait()
            for side in range(2):
                start = (piece * 2 + side) * PIECE
                columns = slice(start, start + PIECE)
                high, low = split(in_buf[phase, side, piece])
                for f in range(6):
                    chosen = chosen_at[f, :, columns]
                    for c in range(3):
                        rows = slice(c * 16, c * 16 + 16)
                        halves[f * 96 + c * 16 : f * 96 + c * 16 + 16, columns] = high[rows] * chosen
                        halves[f * 96 + 48 + c * 16 : f * 96 + 64 + c * 16, columns] = low[rows] * chosen
            both = slice(piece * 2 * PIECE, piece * 2 * PIECE + 2 * PIECE)
            for t in range(0, slots, 256):
                columns = slice(t, t + 256)
                got = dot(halves[:, both], onehot[6, both, columns])
                for f in range(6):
                    total = jump[f, :, columns] + got[f * 96 : f * 96 + 48] + got[f * 96 + 48 : f * 96 + 96]
                    if piece < last:
                        jump[f, :, columns] = total
                        continue
                    high, low = split(total)
                    for c in range(3):
                        jump_in[c, f * 16 : f * 16 + 16, columns] = high[c * 16 : c * 16 + 16]
                        jump_in[c, 96 + f * 16 : 112 + f * 16, columns] = low[c * 16 : c * 16 + 16]

    def put3(ref, index, high, low):
        ref[index, 0:64] = high
        ref[index, 64:128] = high
        ref[index, 128:192] = low

    def put_traces(field, pairs):
        for h in range(0, slots, HALF):
            columns = slice(h, h + HALF)
            tiles = [field[k * 8 : k * 8 + 8, columns] for k in range(8)]
            for c, d in pairs:
                for end, rows in enumerate(face_rows(tiles, d)):
                    high, low = split(jnp.concatenate(rows, axis=0))
                    traces[2 * d + end, c * 16 : c * 16 + 16, columns] = high
                    traces[2 * d + end, 48 + c * 16 : 64 + c * 16, columns] = low

    def velocity_traces():
        for c in range(3):
            put_traces(vel.at[c], [(c, d) for d in range(3)])

    def stress_traces():
        for m, pairs in enumerate(
            (((0, 0),), ((1, 1),), ((2, 2),), ((1, 0), (0, 1)), ((2, 0), (0, 2)), ((2, 1), (1, 2)))
        ):
            put_traces(sig.at[m], pairs)

    blocks = [
        (r, slice(r, r + 8), slice(h, h + HALF)) for r in range(0, 64, 8) for h in range(0, slots, HALF)
    ]

    def step(n, carry):
        velocity_traces()

        send(0, n)

        @pl.when(n == 0)
        def _():
            build_onehot()
            load_s.wait()
            for c in range(6):
                sig[c] = sig[c] * valid
            load_f.wait()

        own(0)
        for c in range(3):
            high, low = split(vel[c])
            put3(field_in, c, high, low)
        for c in range(3):
            high, low = split(forward[n, c])
            fgrad[c] = dot(stage_v[...], jnp.concatenate([high, high, low], axis=0))
            grad[c] = dot(stage_v[...], field_in[c])
        arrive(0)
        for c in range(3):
            got = dot(stage_j[...], jump_in[c])
            impulse[c] = got[0:192]
            kick[c] = got[192:256]
        for r, rows, cols in blocks:
            g = [
                [
                    grad[i, j * 64 + r : j * 64 + r + 8, cols] + impulse[i, j * 64 + r : j * 64 + r + 8, cols]
                    for j in range(3)
                ]
                for i in range(3)
            ]
            shear = mu[rows, cols] * time_step
            bulk = lam[rows, cols] * time_step * (g[0][0] + g[1][1] + g[2][2])
            for c in range(3):
                sig[c, rows, cols] = sig[c, rows, cols] + (bulk + 2.0 * shear * g[c][c])
            for m, (i, j) in ((3, (0, 1)), (4, (0, 2)), (5, (1, 2))):
                sig[m, rows, cols] = sig[m, rows, cols] + shear * (g[i][j] + g[j][i])
        stress_traces()
        send(1, n)
        for r, rows, cols in blocks:
            g = [[fgrad[i, j * 64 + r : j * 64 + r + 8, cols] for j in range(3)] for i in range(3)]
            s = [sig[m, rows, cols] for m in range(6)]
            rate = g[0][0] + g[1][1] + g[2][2]
            acc[1, rows, cols] = acc[1, rows, cols] - time_step * rate * (s[0] + s[1] + s[2])
            contraction = g[0][0] * s[0] + g[1][1] * s[1] + g[2][2] * s[2]
            contraction = contraction + (g[0][1] + g[1][0]) * s[3]
            contraction = contraction + (g[0][2] + g[2][0]) * s[4]
            contraction = contraction + (g[1][2] + g[2][1]) * s[5]
            acc[2, rows, cols] = acc[2, rows, cols] - (2.0 * time_step) * contraction

        if SUM_EVENTS:
            @pl.when(n == steps - 1)
            def _():
                for copy in x_copies(0):
                    copy.start()

        own(1)
        for m in range(6):
            high, low = split(sig[m])
            put3(sig_in, m, high, low)
        for c in range(3):
            total = dot(stage_v[0:64], sig_in[symmetric_index[c][0]])
            total = total + dot(stage_v[64:128], sig_in[symmetric_index[c][1]])
            total = total + dot(stage_v[128:192], sig_in[symmetric_index[c][2]])
            div[c] = total
        arrive(1)
        for c in range(3):
            impulse[c, 0:64] = dot(lift2[...], jump_in[c])
        for r, rows, cols in blocks:
            z = jnp.sqrt(rho[rows, cols] * (lam[rows, cols] + 2.0 * mu[rows, cols]))
            scale = time_step / rho[rows, cols]
            total = jnp.zeros_like(z)
            for c in range(3):
                rate = div[c, rows, cols] + impulse[c, rows, cols] + z * kick[c, rows, cols]
                new = vel[c, rows, cols] + scale * rate
                vel[c, rows, cols] = new
                total = total + forward[n, c, rows, cols] * new
            acc[0, rows, cols] = acc[0, rows, cols] - time_step * total
        return carry

    valid = jnp.where(jnp.max(near[...], axis=0, keepdims=True) >= 0, 1.0, 0.0)
    load_v.wait()
    for c in range(3):
        vel[c] = vel[c] * valid
    lax.fori_loop(0, steps, step, 0)
    store_v = pltpu.make_async_copy(vel, vel_hbm.at[0], load_sem.at[0])
    if SUM_EVENTS:
        for copy in x_copies(1):
            copy.start()
    store_v.start()
    if SUM_EVENTS:
        scatter_on(0)
        scatter_on(1)
        gather_in(0)
        gather_in(1)
    else:
        part[...] = acc[...]
    store_v.wait()


def hand_out(vel_in, part_in, vel_out, part_out, vel, part, sem):
    loads = [pltpu.make_async_copy(vel_in.at[0, c], vel.at[c], sem.at[0, c]) for c in range(3)]
    loads.append(pltpu.make_async_copy(part_in, part, sem.at[0, 3]))
    stores = [pltpu.make_async_copy(vel.at[c], vel_out.at[0, c], sem.at[1, c]) for c in range(3)]
    stores.append(pltpu.make_async_copy(part, part_out, sem.at[1, 3]))
    for copy in loads:
        copy.start()
    for load, store in zip(loads, stores):
        load.wait()
        store.start()
    for copy in stores:
        copy.wait()


def local(
    adjoint_state, forward_velocity, density, lame_lambda, shear_modulus, neighbour, send_list
):
    slots = density.shape[1]
    stage_v, stage_j, lift2 = (jnp.asarray(x) for x in tables())
    vmem = pl.BlockSpec(memory_space=pltpu.VMEM)
    hbm = pl.BlockSpec(memory_space=pl.ANY)
    share = 64 * slots // (NX * NZ)
    steps = forward_velocity.shape[1]
    velocity, part = pl.pallas_call(
        sim_kernel,
        out_shape=(
            jax.ShapeDtypeStruct((1, 3, 64, slots), f32),
            jax.ShapeDtypeStruct((3, 1, share) if SUM_EVENTS else (3, 64, slots), f32),
        ),
        in_specs=[hbm] * 2 + [vmem] * 8,
        out_specs=(hbm, vmem),
        scratch_shapes=[
            pltpu.VMEM((3, 64, slots), f32),
            pltpu.VMEM((steps, 3, 64, slots), f32),
            pltpu.VMEM((3, 64, slots), f32),
            pltpu.VMEM((6, 64, slots), f32),
            pltpu.VMEM((7, 2 * SIDE, slots), bf16),
            pltpu.VMEM((slots, 2 * SIDE), bf16),
            pltpu.VMEM((2, 16, 2 * SIDE), bf16),
            pltpu.VMEM((6, 16, slots), bf16),
            pltpu.VMEM((6, 16, slots), bf16),
            pltpu.VMEM((6, 16, slots), bf16),
            pltpu.VMEM((6, 16, slots), bf16),
            pltpu.VMEM((8, 2 * SIDE), jnp.int32),
            pltpu.VMEM((6, 96, slots), bf16),
            pltpu.VMEM((6, 48, slots), f32),
            pltpu.VMEM((3, 192, slots), bf16),
            pltpu.VMEM((3, 192, slots), bf16),
            pltpu.VMEM((3, 192, slots), f32),
            pltpu.VMEM((3, 64, slots), f32),
            pltpu.VMEM((3, 192, slots), f32),
            pltpu.VMEM((6, 192, slots), bf16),
            pltpu.VMEM((3, 192, slots), f32),
            pltpu.VMEM((3, 64, slots), f32),
            pltpu.VMEM((576, 2 * SIDE), bf16),
            pltpu.VMEM((6, 16, 2 * SIDE), bf16),
            pltpu.VMEM((2, 2, SIDE // PIECE, 48, PIECE), f32),
            pltpu.VMEM((2, 2, SIDE // PIECE, 48, PIECE), f32),
            pltpu.VMEM((NX - 1, 3, 64 // NX, slots), f32),
            pltpu.VMEM((3, 64 // NX, slots), f32),
            pltpu.VMEM((NZ, 3, share // 128, 128), f32),
            pltpu.VMEM((NZ - 1, 3, share // 128, 128), f32),
            pltpu.SemaphoreType.DMA((3,)),
            pltpu.SemaphoreType.DMA((2, 2, SIDE // PIECE)),
            pltpu.SemaphoreType.DMA((2, 2, SIDE // PIECE)),
            pltpu.SemaphoreType.DMA((2, NX - 1)),
            pltpu.SemaphoreType.DMA((2, NX - 1)),
            pltpu.SemaphoreType.DMA((2, NZ - 1)),
            pltpu.SemaphoreType.DMA((2, NZ - 1)),
        ],
        compiler_params=pltpu.CompilerParams(
            collective_id=0, has_side_effects=True, vmem_limit_bytes=60 * 1024 * 1024
        ),
    )(
        adjoint_state, forward_velocity, density, lame_lambda, shear_modulus, neighbour, send_list,
        stage_v, stage_j, lift2,
    )
    if not SUM_EVENTS:
        part = part.reshape(3, 1, -1)
    return pl.pallas_call(
        hand_out,
        out_shape=tuple(jax.ShapeDtypeStruct(x.shape, f32) for x in (velocity, part)),
        in_specs=[hbm, hbm],
        out_specs=(hbm, hbm),
        scratch_shapes=[
            pltpu.VMEM(velocity.shape[1:], f32),
            pltpu.VMEM(part.shape, f32),
            pltpu.SemaphoreType.DMA((2, 4)),
        ],
    )(velocity, part)


def solution(mesh):
    placed = (
        P("event", None, None, "dom"),
        P("event", None, None, None, "dom"),
        P(None, "dom"),
        P(None, "dom"),
        P(None, "dom"),
        P(None, "dom"),
        P(None, "dom"),
    )
    return jax.shard_map(
        local,
        mesh=mesh,
        in_specs=placed,
        out_specs=(P("event", None, None, "dom"), P(None, "dom", "event")),
        check_vma=False,
    )
```
